128 devices in a mesh: seq: 16 (over y, z_lo, core), chan: 8 (over x, z_hi).
Axes of the slice: x: 4, y: 4, z: 4 (z_hi: 2, z_lo: 2; z = z_hi * 2 + z_lo), core: 2. Of those that a mesh axis runs over, the one named last changes fastest.
Arguments:
- token_ids: int32 [8192], P('seq'), may hold values from 0 to 511
- embed_table: bfloat16 [512, 4096], replicated, may hold values from -6 to 6
- in_weight: bfloat16 [4096, 3, 2048], P(None, None, 'chan'), may hold values from -0.09375 to 0.09375
- short_filter: float32 [3, 3, 2048], P(None, None, 'chan'), may hold values from -3 to 3
- long_filter: float32 [8192, 2048], P('seq', 'chan'), may hold values from -1.5 to 1.5
- skip_gain: float32 [2048], P('chan'), may hold values from -4 to 4
- out_weight: bfloat16 [2048, 4096], P('chan'), may hold values from -0.125 to 0.125
Outputs:
- mixed: bfloat16 [8192, 4096], P(('seq', 'chan'))
The draws below stay inside these ranges and needn't reach their ends.
All inputs are finite; a program needn't handle non-finite values.
Results may differ from the reference program's by a relative error of at most 0.0072.
Values may be sent and summed in bfloat16 or wider, within the bound.
No kernel may reach another device: no remote copies, remote signals or barrier semaphores. Data moves between devices by JAX's collectives and lax.ppermute only.
A program may use at most 128 MiB of HBM per device.

```python
import math
import jax
import jax.numpy as jnp
import numpy as np

D = 4096
VOCAB = 512
OPERATOR_WIDTH = 2048
TAPS = 3
SEQUENCE_LENGTH = 8192


def draw_long_filter(key, part):
    noise_key = jax.random.fold_in(key, 11)
    rate_key = jax.random.fold_in(key, 12)
    pulse_key = jax.random.fold_in(key, 13)
    delay_positions = jnp.arange(SEQUENCE_LENGTH, dtype=jnp.float32)[:, None]
    log_time = jax.random.uniform(rate_key, (OPERATOR_WIDTH,), jnp.float32, math.log(30.0), math.log(4.0 * SEQUENCE_LENGTH))
    noise_field = jnp.clip(jax.random.normal(noise_key, (SEQUENCE_LENGTH, OPERATOR_WIDTH), jnp.float32), -5.0, 5.0)
    decay_length = jnp.exp(log_time)
    pulse_delays = jax.random.uniform(pulse_key, (3, OPERATOR_WIDTH), jnp.float32, 0.0, 1.0 * SEQUENCE_LENGTH)
    pulse_count = jnp.zeros((SEQUENCE_LENGTH, OPERATOR_WIDTH), jnp.float32)
    for pulse_index in range(3):
        pulse_count = pulse_count + (delay_positions >= pulse_delays[pulse_index][None, :]).astype(jnp.float32)
    envelope = jnp.exp(-delay_positions / decay_length[None, :]) + 0.03
    decay_curve = envelope * jnp.power(0.6, pulse_count)
    scale_factor = 1.0 / jnp.sqrt(jnp.minimum(0.5 * decay_length, 1.0 * SEQUENCE_LENGTH) + 1.0)
    return noise_field * decay_curve * scale_factor[None, :]


def with_ends(result, rng, smallest, largest):
    index_at = [jax.random.randint(jax.random.fold_in(rng, axis), (), 0, length) for axis, length in enumerate(result.shape)]
    main_axis = result.shape.index(max(result.shape))
    next_to = index_at[:main_axis] + [(index_at[main_axis] + 1) % result.shape[main_axis]] + index_at[main_axis + 1:]
    return result.at[tuple(index_at)].set(smallest).at[tuple(next_to)].set(largest)


def block_scale(key, shape, split, smallest, largest):
    factor_of = 1.0
    for position, blocks in split:
        draws = jax.random.uniform(jax.random.fold_in(jax.random.fold_in(key, 6), position), (blocks,), jnp.float32, smallest / len(split), largest / len(split))
        factor_of = factor_of * jnp.repeat(jnp.exp(draws), shape[position] // blocks).reshape((-1,) + (1,) * (len(shape) - 1 - position))
    return factor_of


def rank_bounds(amount, skew):
    weights = [(1 << 20) // math.isqrt(standing ** skew) + 1 for standing in range(1, amount + 1)]
    scale = 1 + sum(weights) // (1 << 30)
    return np.cumsum(np.array([max(1, weight // scale) for weight in weights]))


def skewed_ids(key, extent, number_of, skew):
    grid = rank_bounds(number_of, skew)
    pick = jax.random.randint(jax.random.fold_in(key, 1), extent, 0, int(grid[number_of - 1]))
    rank = jnp.searchsorted(jnp.asarray(grid, jnp.int32), pick, side="right")
    return jax.random.permutation(jax.random.fold_in(key, 2), number_of)[rank].astype(jnp.int32)


def centred(key, shape, width, limit, shards=(), held_as=jnp.bfloat16):
    drawn = width * jax.random.normal(key, shape, jnp.float32)
    if shards:
        drawn = drawn * block_scale(key, shape, shards, -0.22, 0.18)
    return jnp.clip(drawn, -limit, limit).astype(held_as)


def setup_inputs(seed: int = 0) -> dict:
    arg_keys = jax.random.split(jax.random.key(seed), 8)
    token_ids = with_ends(skewed_ids(arg_keys[0], (SEQUENCE_LENGTH,), VOCAB, 2), jax.random.fold_in(arg_keys[0], 3), 0, VOCAB - 1).astype(jnp.int32)
    embed_table = centred(arg_keys[1], (VOCAB, D), 1.0, 6.0)
    in_weight = centred(arg_keys[2], (D, 3, OPERATOR_WIDTH), D ** -0.5, 0.09375, ((2, 8),))
    short_filter = centred(arg_keys[3], (TAPS, 3, OPERATOR_WIDTH), 0.6, 3.0, ((2, 8),), jnp.float32)
    long_filter = draw_long_filter(jax.random.fold_in(arg_keys[7], 71), 0)
    skip_gain = centred(arg_keys[5], (OPERATOR_WIDTH,), 1.0, 4.0, ((0, 8),), jnp.float32)
    out_weight = centred(arg_keys[6], (OPERATOR_WIDTH, D), OPERATOR_WIDTH ** -0.5, 0.125, ((0, 8),))
    return dict(token_ids=token_ids, embed_table=embed_table, in_weight=in_weight, short_filter=short_filter, long_filter=long_filter, skip_gain=skip_gain, out_weight=out_weight)


def reference(token_ids, embed_table, in_weight, short_filter, long_filter, skip_gain, out_weight):
    embedded = jnp.take(embed_table, token_ids, axis=0)
    weights_flat = in_weight.reshape(in_weight.shape[0], -1)
    projected = jnp.dot(embedded, weights_flat, preferred_element_type=jnp.float32).astype(jnp.bfloat16)
    row_count = embedded.shape[0]
    projected = projected.reshape(row_count, 3, -1)
    tap_count = short_filter.shape[0]
    padded = jnp.concatenate([jnp.zeros((tap_count - 1,) + projected.shape[1:], jnp.bfloat16), projected], 0)
    filtered = jnp.zeros(projected.shape, jnp.float32)
    for tap_index in range(tap_count):
        start_row = tap_count - 1 - tap_index
        filtered = filtered + short_filter[tap_index] * padded[start_row:start_row + row_count].astype(jnp.float32)
    gated_value = filtered[:, 0] * filtered[:, 2]
    full_len = 2 * row_count
    spectrum = jnp.fft.rfft(gated_value, n=full_len, axis=0) * jnp.fft.rfft(long_filter, n=full_len, axis=0)
    convolved = jnp.fft.irfft(spectrum, n=full_len, axis=0)[:row_count]
    carried = (filtered[:, 1] * (convolved + skip_gain * gated_value)).astype(jnp.bfloat16)
    return jnp.dot(carried, out_weight, preferred_element_type=jnp.float32).astype(jnp.bfloat16)
```

```python
import functools
import itertools
import math

import jax
import jax.numpy as jnp
import ml_dtypes
import numpy as np
from jax import lax
from jax.experimental import pallas as pl
from jax.experimental.pallas import tpu as pltpu
from jax.sharding import Mesh
from jax.sharding import PartitionSpec as P


SIZES = {"y": 4, "zl": 2, "core": 2, "x": 4, "zh": 2}
AXES = tuple(SIZES)
SEQ, CHAN = ("y", "zl", "core"), ("x", "zh")

N1 = 128
HALF = 72
CH = 16
BF, F32 = jnp.bfloat16, jnp.float32


def split_np(array):
    high = array.astype(np.float32).astype(ml_dtypes.bfloat16)
    low = (array - high.astype(np.float64)).astype(np.float32).astype(ml_dtypes.bfloat16)
    return high, low


@functools.cache
def tables():
    full = 2 * 8192
    freq = np.arange(HALF)[:, None]
    valid = (freq <= N1 // 2).astype(np.float64)
    block = np.arange(64)[None, :]
    angle = 2 * np.pi * (freq * block % N1) / N1
    first = np.concatenate([np.cos(angle) * valid, -np.sin(angle) * valid], 0)
    high, low = split_np(first)
    zero = np.zeros_like(high)
    first_signal = np.concatenate([high, high, low, zero], 1)
    rank = np.arange(64)
    order = 4 * (rank % 16) + rank // 16
    first_filter = np.concatenate([high[:, order], low[:, order]], 1)
    lane = np.arange(128)[None, :]
    turn = 2 * np.pi * (freq * lane) / full
    twiddle = np.stack([np.cos(turn) * valid, -np.sin(turn) * valid]).astype(np.float32)
    pair = 2 * np.pi * (np.arange(128)[:, None] * lane % 128) / 128
    cosine, sine = np.cos(pair), np.sin(pair)
    second = np.concatenate(
        [np.concatenate([cosine, -sine], 1), np.concatenate([sine, cosine], 1)], 0
    )
    second = np.stack(split_np(second))
    weight = np.where((freq == 0) | (freq == N1 // 2), 1.0, 2.0) * valid / full
    last = np.concatenate([np.cos(angle) * weight, -np.sin(angle) * weight], 0).T
    high, low = split_np(last)
    last = np.concatenate([high, high, low, np.zeros((64, 80), high.dtype)], 1)
    return first_signal, first_filter, twiddle, second, last


def halves(value):
    high = value.astype(BF)
    return high, (value - high.astype(F32)).astype(BF)


def mm(left, right, dims=(((1,), (0,)), ((), ()))):
    return lax.dot_general(left, right, dims, preferred_element_type=F32)


def prepare_kernel(where, embed, weight, filt, tokens, table, payload, acc):
    step = pl.program_id(0)
    wide = jnp.concatenate([weight[0], weight[1], weight[2]], 1)
    part = mm(embed[...], wide)

    @pl.when(step == 0)
    def _():
        acc[...] = part
        payload[:, :, :512] = filt[...].T.astype(BF).reshape(16, CH, 512)
        high = jnp.right_shift(tokens[...], 4)
        low = jnp.bitwise_and(tokens[...], 15)
        gap = jnp.zeros((4, 128), F32)
        digits = jnp.concatenate([high.astype(F32), gap, low.astype(F32), gap], 0).astype(BF)
        payload[:, :, 512:] = jnp.broadcast_to(digits[None], (16, CH, 128))

    @pl.when(step > 0)
    def _():
        acc[...] += part

    @pl.when(step == pl.num_programs(0) - 1)
    def _():
        lane = lax.broadcasted_iota(jnp.int32, (CH, 128), 1)
        row = lax.broadcasted_iota(jnp.int32, (CH, 128), 0)
        pick = (lane == row + CH * where[1]).astype(F32).astype(BF)
        for branch in range(3):
            rows = acc[:, branch * 128 : (branch + 1) * 128].astype(BF)
            table[branch * CH : (branch + 1) * CH, :] = mm(pick, rows, (((1,), (1,)), ((), ())))


def prepare(seq, embed_table, in_weight, long_filter, token_ids):
    steps = 8
    depth = in_weight.shape[0] // steps
    where = jnp.stack([seq // 8, seq % 8]).astype(jnp.int32)
    return pl.pallas_call(
        prepare_kernel,
        out_shape=(
            jax.ShapeDtypeStruct((3 * CH, 512), F32),
            jax.ShapeDtypeStruct((16, CH, 640), BF),
        ),
        grid_spec=pltpu.PrefetchScalarGridSpec(
            num_scalar_prefetch=1,
            grid=(steps,),
            in_specs=[
                pl.BlockSpec((512, depth), lambda i, w: (0, i)),
                pl.BlockSpec((3, depth, 128), lambda i, w: (0, i, w[0])),
                pl.BlockSpec((512, 256), lambda i, w: (0, 0)),
                pl.BlockSpec((4, 128), lambda i, w: (0, 0)),
            ],
            out_specs=(
                pl.BlockSpec((3 * CH, 512), lambda i, w: (0, 0)),
                pl.BlockSpec((16, CH, 640), lambda i, w: (0, 0, 0)),
            ),
            scratch_shapes=[pltpu.VMEM((512, 384), F32)],
        ),
        compiler_params=pltpu.CompilerParams(dimension_semantics=("arbitrary",)),
        cost_estimate=pl.CostEstimate(flops=2 * 512 * 4096 * 384, bytes_accessed=8 << 20, transcendentals=0),
        name="prepare",
    )(where, embed_table, in_weight.transpose(1, 0, 2), long_filter, token_ids.reshape(4, 128))


def convolve_kernel(
    where, recv, table, coef, first_signal, first_filter, twiddle, second, last,
    out, taps, token, gated, other, shaped, spec_high, spec_low, lags,
):
    seq, core = where[0], where[1]
    lane = lax.broadcasted_iota(jnp.int32, (CH, 256), 1)
    row = lax.broadcasted_iota(jnp.int32, (CH, 256), 0)
    mine = lane == row + CH * seq
    for index in range(10):
        column = jnp.sum(jnp.where(mine, coef[index : index + 1, :], 0.0), axis=1, keepdims=True)
        taps[index * CH : (index + 1) * CH, :] = jnp.broadcast_to(column, (CH, 128))

    for source in range(16):
        digits = recv[source, :, 512:].astype(F32)
        token[source * 8 : source * 8 + 8, :] = (digits[:8] * 16.0 + digits[8:]).astype(jnp.int32)
        for q in range(4):
            rows = slice(q * 256 + source * CH, q * 256 + (source + 1) * CH)
            lags[rows, :] = recv[source, :, q * 128 : (q + 1) * 128].astype(F32)

    position = lax.broadcasted_iota(jnp.int32, (3 * CH, 128), 1)

    def select(source, carried):
        before_one, before_two = carried
        for quarter in range(4):
            ids = jnp.broadcast_to(token[pl.ds(source * 8 + quarter, 1), :], (3 * CH, 128))
            place = jnp.bitwise_and(ids, 127)
            bank = jnp.right_shift(ids, 7)
            value = None
            for index in range(4):
                found = jnp.take_along_axis(
                    table[:, index * 128 : (index + 1) * 128], place, axis=1, mode="promise_in_bounds"
                )
                value = found if index == 0 else jnp.where(bank == index, found, value)
            one = pltpu.roll(value, 1, 1)
            two = pltpu.roll(value, 2, 1)
            lag_one = jnp.where(position < 1, before_one, one)
            lag_two = jnp.where(position < 2, before_two, two)
            before_one, before_two = one, two
            filtered = taps[: 3 * CH, :] * value
            filtered = filtered + taps[3 * CH : 6 * CH, :] * lag_one
            filtered = filtered + taps[6 * CH : 9 * CH, :] * lag_two
            rows = pl.ds(pl.multiple_of((source * 4 + quarter) * CH, CH), CH)
            gated[rows, :] = filtered[:CH] * filtered[2 * CH :]
            other[rows, :] = filtered[CH : 2 * CH]
        return before_one, before_two

    nothing = jnp.zeros((3 * CH, 128), F32)
    lax.fori_loop(0, 16, select, (nothing, nothing))

    cos_turn, sin_turn = twiddle[0], twiddle[1]
    rows_all = CH * HALF

    def turned(stage, sign):
        real, imag = stage[:HALF], stage[HALF:]
        return jnp.concatenate(
            [real * cos_turn - sign * imag * sin_turn, sign * real * sin_turn + imag * cos_turn], 1
        )

    for pair in range(CH // 2):
        signal = jnp.concatenate(
            [gated[pl.ds(2 * pair + i, 64, stride=CH), :] for i in range(2)], 1
        )
        high, low = halves(signal)
        stage = mm(first_signal[...], jnp.concatenate([high, low, high, high], 0))
        spectrum = jnp.concatenate([turned(stage[:, :128], 1), turned(stage[:, 128:], 1)], 0)
        at = slice(pair * 2 * HALF, (pair + 1) * 2 * HALF)
        spec_high[at, :], spec_low[at, :] = halves(spectrum)

        kernel = jnp.concatenate(
            [lags[pl.ds(2 * pair + i, 64, stride=CH), :] for i in range(2)], 1
        ).astype(BF)
        stage = mm(first_filter[...], jnp.concatenate([kernel, kernel], 0))
        spectrum = jnp.concatenate([turned(stage[:, :128], 1), turned(stage[:, 128:], 1)], 0)
        at = slice(rows_all + pair * 2 * HALF, rows_all + (pair + 1) * 2 * HALF)
        spec_high[at, :], spec_low[at, :] = halves(spectrum)

    def transform(at, dims):
        high, low = spec_high[at, :], spec_low[at, :]
        return mm(high, second[0], dims) + (mm(low, second[0], dims) + mm(high, second[1], dims))

    straight, flipped = (((1,), (0,)), ((), ())), (((1,), (1,)), ((), ()))
    for pair in range(CH // 2):
        at = slice(pair * 2 * HALF, (pair + 1) * 2 * HALF)
        left = transform(at, straight)
        right = transform(slice(rows_all + at.start, rows_all + at.stop), straight)
        left_real, left_imag, right_real, right_imag = left[:, :128], left[:, 128:], right[:, :128], right[:, 128:]
        product = jnp.concatenate(
            [left_real * right_real - left_imag * right_imag, left_real * right_imag + left_imag * right_real], 1
        )
        spec_high[at, :], spec_low[at, :] = halves(product)

    for pair in range(CH // 2):
        at = slice(pair * 2 * HALF, (pair + 1) * 2 * HALF)
        back = transform(at, flipped)
        columns = []
        for i in range(2):
            part = back[i * HALF : (i + 1) * HALF]
            real, imag = part[:, :128], part[:, 128:]
            columns.append(
                jnp.concatenate([real * cos_turn + imag * sin_turn, imag * cos_turn - real * sin_turn], 0)
            )
        high, low = halves(jnp.concatenate(columns, 1))
        result = mm(last[...], jnp.concatenate([high, low, high, high[:80]], 0))
        for i in range(2):
            shaped[pl.ds(2 * pair + i, 64, stride=CH), :] = result[:, i * 128 : (i + 1) * 128]

    skip = taps[9 * CH :, :]
    low_half = lax.broadcasted_iota(jnp.int32, (CH, 128), 1) < 64
    for a, top, core_to, h in itertools.product(range(2), range(2), range(2), range(4)):
        done = []
        for zl in range(2):
            shard = 8 * a + top * 4 + zl * 2 + core_to
            rows = slice((4 * shard + h) * CH, (4 * shard + h + 1) * CH)
            done.append(other[rows, :] * (shaped[rows, :] + skip * gated[rows, :]))
        first, then = done
        even = jnp.where(low_half, first, pltpu.roll(then, 64, 1)).astype(BF)
        odd = jnp.where(low_half, pltpu.roll(first, 64, 1), then).astype(BF)
        half = jnp.bitwise_xor(core, core_to) if core_to else core
        columns = pl.ds(pl.multiple_of(half * 256 + top * 128, 128), 128)
        for to_y, to_z in itertools.product(range(2), range(2)):
            out[a, to_y, to_z, 2 * h, :, columns] = even
            out[a, to_y, to_z, 2 * h + 1, :, columns] = odd


def convolve(seq, core, recv, table, coef):
    consts = [jnp.asarray(c) for c in tables()]
    where = jnp.stack([seq, core]).astype(jnp.int32)
    whole = pl.BlockSpec(memory_space=pltpu.VMEM)
    positions = 8192
    return pl.pallas_call(
        convolve_kernel,
        out_shape=jax.ShapeDtypeStruct((2, 2, 2, 8, CH, 512), BF),
        in_specs=[pl.BlockSpec(memory_space=pltpu.SMEM)] + [whole] * 8,
        out_specs=whole,
        scratch_shapes=[
            pltpu.VMEM((10 * CH, 128), F32),
            pltpu.VMEM((128, 128), jnp.int32),
            pltpu.VMEM((positions // 128 * CH, 128), F32),
            pltpu.VMEM((positions // 128 * CH, 128), F32),
            pltpu.VMEM((positions // 128 * CH, 128), F32),
            pltpu.VMEM((2 * CH * HALF, 256), BF),
            pltpu.VMEM((2 * CH * HALF, 256), BF),
            pltpu.VMEM((64 * CH, 128), F32),
        ],
        cost_estimate=pl.CostEstimate(flops=4 << 30, bytes_accessed=4 << 20, transcendentals=0),
        name="convolve",
    )(where, recv, table, coef, *consts)


def project_kernel(where, recv, *refs):
    weights, keep, send = refs[:8], refs[8], refs[9]
    total = None
    for pair in range(4):
        lhs = jnp.concatenate(
            [recv[:, jnp.bitwise_xor(where[0], 2 * pair + i)].reshape(128, 512) for i in range(2)], 0
        )
        rhs = jnp.concatenate([weights[2 * pair + i][...] for i in range(2)], 0)
        part = mm(lhs, rhs, (((0,), (0,)), ((), ())))
        total = part if total is None else total + part
    keep[...] = total[:256]
    send[...] = total[256:].astype(BF)


def project(chan, recv, weights):
    whole = pl.BlockSpec(memory_space=pltpu.VMEM)
    return pl.pallas_call(
        project_kernel,
        out_shape=(jax.ShapeDtypeStruct((256, 1024), F32), jax.ShapeDtypeStruct((256, 1024), BF)),
        in_specs=[pl.BlockSpec(memory_space=pltpu.SMEM)] + [whole] * 9,
        out_specs=(whole, whole),
        cost_estimate=pl.CostEstimate(flops=1 << 30, bytes_accessed=5 << 20, transcendentals=0),
        name="project",
    )(chan.reshape(1), recv.reshape(8, 8, CH, 512), *weights)


def combine_kernel(where, keep, came, *outs):
    for index, out in enumerate(outs):
        block = jnp.bitwise_xor(where[0], index)
        rows = pl.ds(pl.multiple_of(block * 64, 64), 64)
        out[...] = (keep[rows, :] + came[rows, :].astype(F32)).astype(BF)


def combine(column, keep, came):
    whole = pl.BlockSpec(memory_space=pltpu.VMEM)
    return pl.pallas_call(
        combine_kernel,
        out_shape=(jax.ShapeDtypeStruct((64, 1024), BF),) * 4,
        in_specs=[pl.BlockSpec(memory_space=pltpu.SMEM), whole, whole],
        out_specs=(whole,) * 4,
        cost_estimate=pl.CostEstimate(flops=1 << 18, bytes_accessed=2 << 20, transcendentals=0),
        name="combine",
    )(column.reshape(1), keep, came)


def assemble_kernel(where, *refs):
    out = refs[-1]
    for index, piece in enumerate(refs[:-1]):
        block = jnp.bitwise_xor(where[0], index)
        out[:, pl.ds(pl.multiple_of(block * 1024, 1024), 1024)] = piece[...]


def assemble(column, pieces):
    whole = pl.BlockSpec(memory_space=pltpu.VMEM)
    return pl.pallas_call(
        assemble_kernel,
        out_shape=jax.ShapeDtypeStruct((64, 4096), BF),
        in_specs=[pl.BlockSpec(memory_space=pltpu.SMEM)] + [whole] * 4,
        out_specs=whole,
        cost_estimate=pl.CostEstimate(flops=0, bytes_accessed=1 << 20, transcendentals=0),
        name="assemble",
    )(column.reshape(1), *pieces)


def permuted(block, move):
    pairs = []
    for place in itertools.product(*[range(SIZES[axis]) for axis in AXES]):
        here = dict(zip(AXES, place))
        there = {**here, **move(here)}
        index = [0, 0]
        for axis in AXES:
            index = [index[0] * SIZES[axis] + here[axis], index[1] * SIZES[axis] + there[axis]]
        pairs.append(tuple(index))
    return lax.ppermute(block, AXES, pairs)


def body(token_ids, embed_table, in_weight, short_filter, long_filter, skip_gain, out_weight):
    y, zl, core = (lax.axis_index(axis) for axis in SEQ)
    x, zh = (lax.axis_index(axis) for axis in CHAN)
    seq = (y * 2 + zl) * 2 + core
    chan = x * 2 + zh
    column = (y % 2) * 2 + zl

    held = out_weight.reshape(8, 2, CH, 4, 1024)
    held = lax.dynamic_slice(held, (0, core, 0, column, 0), (8, 1, CH, 1, 1024)).reshape(128, 1024)
    weights = []
    for index in range(8):
        dx, dz = index // 2, index % 2
        weights.append(
            held if index == 0 else permuted(held, lambda d: {"x": d["x"] ^ dx, "zh": d["zh"] ^ dz})
        )

    table, payload = prepare(seq, embed_table, in_weight, long_filter, token_ids)
    recv = lax.all_to_all(payload, SEQ, 0, 0, tiled=True)
    coef = jnp.concatenate([short_filter.reshape(9, -1), skip_gain[None, :]], 0)
    chunks = convolve(seq, core, recv, table, coef)
    recv = lax.all_to_all(chunks.reshape(64, CH, 512), ("y", "zl", "x", "zh"), 0, 0, tiled=True)
    keep, send = project(chan, recv, weights)
    came = permuted(send, lambda d: {"core": 1 - d["core"]})
    pieces = list(combine(column, keep, came))
    for index in range(1, 4):
        pieces[index] = permuted(
            pieces[index], lambda d: {"y": d["y"] ^ (index // 2), "zl": d["zl"] ^ (index % 2)}
        )
    return assemble(column, pieces)


def solution(mesh):
    fine = Mesh(mesh.devices.reshape(tuple(SIZES.values())), AXES)
    return jax.shard_map(
        body,
        mesh=fine,
        in_specs=(
            P(SEQ),
            P(),
            P(None, None, CHAN),
            P(None, None, CHAN),
            P(SEQ, CHAN),
            P(CHAN),
            P(CHAN, None),
        ),
        out_specs=P(AXES, None),
        check_vma=False,
    )
```

```python
import functools
import itertools

import jax
import jax.numpy as jnp
import ml_dtypes
import numpy as np
from jax import lax
from jax.experimental import pallas as pl
from jax.experimental.pallas import tpu as pltpu
from jax.sharding import Mesh
from jax.sharding import PartitionSpec as P


SIZES = {"y": 4, "zl": 2, "core": 2, "x": 4, "zh": 2}
AXES = tuple(SIZES)
SEQ, CHAN = ("y", "zl", "core"), ("x", "zh")

N1 = 128
HALF = 72
CH = 16
BF, F32 = jnp.bfloat16, jnp.float32


def split_np(array):
    high = array.astype(np.float32).astype(ml_dtypes.bfloat16)
    low = (array - high.astype(np.float64)).astype(np.float32).astype(ml_dtypes.bfloat16)
    return high, low


@functools.cache
def tables():
    full = 2 * 8192
    freq = np.arange(HALF)[:, None]
    valid = (freq <= N1 // 2).astype(np.float64)
    block = np.arange(64)[None, :]
    angle = 2 * np.pi * (freq * block % N1) / N1
    first = np.concatenate([np.cos(angle) * valid, -np.sin(angle) * valid], 0)
    high, low = split_np(first)
    zero = np.zeros_like(high)
    first_signal = np.concatenate([high, high, low, zero], 1)
    rank = np.arange(64)
    order = 4 * (rank % 16) + rank // 16
    first_filter = np.concatenate([high[:, order], low[:, order]], 1)
    lane = np.arange(128)[None, :]
    turn = 2 * np.pi * (freq * lane) / full
    twiddle = np.stack([np.cos(turn) * valid, -np.sin(turn) * valid]).astype(np.float32)
    pair = 2 * np.pi * (np.arange(128)[:, None] * lane % 128) / 128
    cosine, sine = np.cos(pair), np.sin(pair)
    second = np.concatenate(
        [np.concatenate([cosine, -sine], 1), np.concatenate([sine, cosine], 1)], 0
    )
    second = np.stack(split_np(second))
    weight = np.where((freq == 0) | (freq == N1 // 2), 1.0, 2.0) * valid / full
    last = np.concatenate([np.cos(angle) * weight, -np.sin(angle) * weight], 0).T
    high, low = split_np(last)
    last = np.concatenate([high, high, low, np.zeros((64, 80), high.dtype)], 1)
    return first_signal, first_filter, twiddle, second, last


def halves(value):
    high = value.astype(BF)
    return high, (value - high.astype(F32)).astype(BF)


def mm(left, right, dims=(((1,), (0,)), ((), ()))):
    return lax.dot_general(left, right, dims, preferred_element_type=F32)


def seq_index():
    return (lax.axis_index("y") * 2 + lax.axis_index("zl")) * 2 + lax.axis_index("core")


def chan_index():
    return lax.axis_index("x") * 2 + lax.axis_index("zh")


def column_index():
    return lax.rem(lax.axis_index("y"), 2) * 2 + lax.axis_index("zl")


def pack_kernel(filt, tokens, payload):
    payload[:, :, :512] = filt[...].T.astype(BF).reshape(16, CH, 512)
    high = jnp.right_shift(tokens[...], 4)
    low = jnp.bitwise_and(tokens[...], 15)
    gap = jnp.zeros((4, 128), F32)
    digits = jnp.concatenate([high.astype(F32), gap, low.astype(F32), gap], 0).astype(BF)
    payload[:, :, 512:] = jnp.broadcast_to(digits[None], (16, CH, 128))


def pack(long_filter, token_ids):
    whole = pl.BlockSpec(memory_space=pltpu.VMEM)
    return pl.pallas_call(
        pack_kernel,
        out_shape=jax.ShapeDtypeStruct((16, CH, 640), BF),
        in_specs=[whole, whole],
        out_specs=whole,
        cost_estimate=pl.CostEstimate(flops=1 << 18, bytes_accessed=1 << 20, transcendentals=0),
        name="pack",
    )(long_filter, token_ids.reshape(4, 128))


def vocab_kernel(embed, weight, table, acc):
    step = pl.program_id(0)
    wide = jnp.concatenate([weight[0], weight[1], weight[2]], 1)
    part = mm(embed[...], wide)

    @pl.when(step == 0)
    def _():
        acc[...] = part

    @pl.when(step > 0)
    def _():
        acc[...] += part

    @pl.when(step == pl.num_programs(0) - 1)
    def _():
        lane = lax.broadcasted_iota(jnp.int32, (CH, 128), 1)
        row = lax.broadcasted_iota(jnp.int32, (CH, 128), 0)
        pick = (lane == row + CH * lax.rem(seq_index(), 8)).astype(F32).astype(BF)
        for branch in range(3):
            rows = acc[:, branch * 128 : (branch + 1) * 128].astype(BF)
            table[branch * CH : (branch + 1) * CH, :] = mm(pick, rows, (((1,), (1,)), ((), ())))


def vocab(embed_table, in_weight):
    steps = 8
    depth = in_weight.shape[0] // steps
    return pl.pallas_call(
        vocab_kernel,
        out_shape=jax.ShapeDtypeStruct((3 * CH, 512), F32),
        grid_spec=pltpu.PrefetchScalarGridSpec(
            num_scalar_prefetch=0,
            grid=(steps,),
            in_specs=[
                pl.BlockSpec((512, depth), lambda i: (0, i)),
                pl.BlockSpec((3, depth, 128), lambda i: (0, i, lax.div(seq_index(), 8))),
            ],
            out_specs=pl.BlockSpec((3 * CH, 512), lambda i: (0, 0)),
            scratch_shapes=[pltpu.VMEM((512, 384), F32)],
        ),
        compiler_params=pltpu.CompilerParams(dimension_semantics=("arbitrary",)),
        cost_estimate=pl.CostEstimate(flops=2 * 512 * 4096 * 384, bytes_accessed=8 << 20, transcendentals=0),
        name="vocab",
    )(embed_table, in_weight.transpose(1, 0, 2))


def convolve_kernel(
    recv, table, short, direct, first_signal, first_filter, twiddle, second, last,
    out, taps, token, gated, other, shaped, spec_high, spec_low, lags,
):
    seq, core = seq_index(), lax.axis_index("core")
    lane = lax.broadcasted_iota(jnp.int32, (CH, 256), 1)
    row = lax.broadcasted_iota(jnp.int32, (CH, 256), 0)
    mine = lane == row + CH * seq
    for index in range(10):
        wide = short[index // 3, index % 3 : index % 3 + 1, :] if index < 9 else direct[...]
        column = jnp.sum(jnp.where(mine, wide, 0.0), axis=1, keepdims=True)
        taps[index * CH : (index + 1) * CH, :] = jnp.broadcast_to(column, (CH, 128))

    for source in range(16):
        digits = recv[source, :, 512:].astype(F32)
        token[source * 8 : source * 8 + 8, :] = (digits[:8] * 16.0 + digits[8:]).astype(jnp.int32)
        for q in range(4):
            rows = slice(q * 256 + source * CH, q * 256 + (source + 1) * CH)
            lags[rows, :] = recv[source, :, q * 128 : (q + 1) * 128].astype(F32)

    position = lax.broadcasted_iota(jnp.int32, (3 * CH, 128), 1)

    def select(source, carried):
        before_one, before_two = carried
        for quarter in range(4):
            ids = jnp.broadcast_to(token[pl.ds(source * 8 + quarter, 1), :], (3 * CH, 128))
            place = jnp.bitwise_and(ids, 127)
            bank = jnp.right_shift(ids, 7)
            value = None
            for index in range(4):
                found = jnp.take_along_axis(
                    table[:, index * 128 : (index + 1) * 128], place, axis=1, mode="promise_in_bounds"
                )
                value = found if index == 0 else jnp.where(bank == index, found, value)
            one = pltpu.roll(value, 1, 1)
            two = pltpu.roll(value, 2, 1)
            lag_one = jnp.where(position < 1, before_one, one)
            lag_two = jnp.where(position < 2, before_two, two)
            before_one, before_two = one, two
            filtered = taps[: 3 * CH, :] * value
            filtered = filtered + taps[3 * CH : 6 * CH, :] * lag_one
            filtered = filtered + taps[6 * CH : 9 * CH, :] * lag_two
            rows = pl.ds(pl.multiple_of((source * 4 + quarter) * CH, CH), CH)
            gated[rows, :] = filtered[:CH] * filtered[2 * CH :]
            other[rows, :] = filtered[CH : 2 * CH]
        return before_one, before_two

    nothing = jnp.zeros((3 * CH, 128), F32)
    lax.fori_loop(0, 16, select, (nothing, nothing))

    cos_turn, sin_turn = twiddle[0], twiddle[1]
    rows_all = CH * HALF

    def turned(stage, sign):
        real, imag = stage[:HALF], stage[HALF:]
        return jnp.concatenate(
            [real * cos_turn - sign * imag * sin_turn, sign * real * sin_turn + imag * cos_turn], 1
        )

    for pair in range(CH // 2):
        signal = jnp.concatenate(
            [gated[pl.ds(2 * pair + i, 64, stride=CH), :] for i in range(2)], 1
        )
        high, low = halves(signal)
        stage = mm(first_signal[...], jnp.concatenate([high, low, high, high], 0))
        spectrum = jnp.concatenate([turned(stage[:, :128], 1), turned(stage[:, 128:], 1)], 0)
        at = slice(pair * 2 * HALF, (pair + 1) * 2 * HALF)
        spec_high[at, :], spec_low[at, :] = halves(spectrum)

        kernel = jnp.concatenate(
            [lags[pl.ds(2 * pair + i, 64, stride=CH), :] for i in range(2)], 1
        ).astype(BF)
        stage = mm(first_filter[...], jnp.concatenate([kernel, kernel], 0))
        spectrum = jnp.concatenate([turned(stage[:, :128], 1), turned(stage[:, 128:], 1)], 0)
        at = slice(rows_all + pair * 2 * HALF, rows_all + (pair + 1) * 2 * HALF)
        spec_high[at, :], spec_low[at, :] = halves(spectrum)

    def transform(at, dims):
        high, low = spec_high[at, :], spec_low[at, :]
        return mm(high, second[0], dims) + (mm(low, second[0], dims) + mm(high, second[1], dims))

    straight, flipped = (((1,), (0,)), ((), ())), (((1,), (1,)), ((), ()))
    for pair in range(CH // 2):
        at = slice(pair * 2 * HALF, (pair + 1) * 2 * HALF)
        left = transform(at, straight)
        right = transform(slice(rows_all + at.start, rows_all + at.stop), straight)
        left_real, left_imag, right_real, right_imag = left[:, :128], left[:, 128:], right[:, :128], right[:, 128:]
        product = jnp.concatenate(
            [left_real * right_real - left_imag * right_imag, left_real * right_imag + left_imag * right_real], 1
        )
        spec_high[at, :], spec_low[at, :] = halves(product)

    for pair in range(CH // 2):
        at = slice(pair * 2 * HALF, (pair + 1) * 2 * HALF)
        back = transform(at, flipped)
        columns = []
        for i in range(2):
            part = back[i * HALF : (i + 1) * HALF]
            real, imag = part[:, :128], part[:, 128:]
            columns.append(
                jnp.concatenate([real * cos_turn + imag * sin_turn, imag * cos_turn - real * sin_turn], 0)
            )
        high, low = halves(jnp.concatenate(columns, 1))
        result = mm(last[...], jnp.concatenate([high, low, high, high[:80]], 0))
        for i in range(2):
            shaped[pl.ds(2 * pair + i, 64, stride=CH), :] = result[:, i * 128 : (i + 1) * 128]

    skip = taps[9 * CH :, :]
    low_half = lax.broadcasted_iota(jnp.int32, (CH, 128), 1) < 64
    for a, top, core_to, h in itertools.product(range(2), range(2), range(2), range(4)):
        done = []
        for zl in range(2):
            shard = 8 * a + top * 4 + zl * 2 + core_to
            rows = slice((4 * shard + h) * CH, (4 * shard + h + 1) * CH)
            done.append(other[rows, :] * (shaped[rows, :] + skip * gated[rows, :]))
        first, then = done
        even = jnp.where(low_half, first, pltpu.roll(then, 64, 1)).astype(BF)
        odd = jnp.where(low_half, pltpu.roll(first, 64, 1), then).astype(BF)
        half = jnp.bitwise_xor(core, core_to) if core_to else core
        columns = pl.ds(pl.multiple_of(half * 256 + top * 128, 128), 128)
        for to_y, to_z in itertools.product(range(2), range(2)):
            out[a, to_y, to_z, 2 * h, :, columns] = even
            out[a, to_y, to_z, 2 * h + 1, :, columns] = odd


def convolve(recv, table, short_filter, skip_gain):
    consts = [jnp.asarray(c) for c in tables()]
    whole = pl.BlockSpec(memory_space=pltpu.VMEM)
    positions = 8192
    return pl.pallas_call(
        convolve_kernel,
        out_shape=jax.ShapeDtypeStruct((2, 2, 2, 8, CH, 512), BF),
        in_specs=[whole] * 9,
        out_specs=whole,
        scratch_shapes=[
            pltpu.VMEM((10 * CH, 128), F32),
            pltpu.VMEM((128, 128), jnp.int32),
            pltpu.VMEM((positions // 128 * CH, 128), F32),
            pltpu.VMEM((positions // 128 * CH, 128), F32),
            pltpu.VMEM((positions // 128 * CH, 128), F32),
            pltpu.VMEM((2 * CH * HALF, 256), BF),
            pltpu.VMEM((2 * CH * HALF, 256), BF),
            pltpu.VMEM((64 * CH, 128), F32),
        ],
        cost_estimate=pl.CostEstimate(flops=4 << 30, bytes_accessed=4 << 20, transcendentals=0),
        name="convolve",
    )(recv, table, short_filter, skip_gain[None, :], *consts)


def project_kernel(recv, *refs):
    weights, keep, send = refs[:8], refs[8], refs[9]
    total = None
    for pair in range(4):
        lhs = jnp.concatenate(
            [recv[:, jnp.bitwise_xor(chan_index(), 2 * pair + i)].reshape(128, 512) for i in range(2)], 0
        )
        rhs = jnp.concatenate([weights[2 * pair + i][...] for i in range(2)], 0)
        part = mm(lhs, rhs, (((0,), (0,)), ((), ())))
        total = part if total is None else total + part
    keep[...] = total[:256]
    send[...] = total[256:].astype(BF)


def project(recv, weights):
    whole = pl.BlockSpec(memory_space=pltpu.VMEM)
    return pl.pallas_call(
        project_kernel,
        out_shape=(jax.ShapeDtypeStruct((256, 1024), F32), jax.ShapeDtypeStruct((256, 1024), BF)),
        in_specs=[whole] * 9,
        out_specs=(whole, whole),
        cost_estimate=pl.CostEstimate(flops=1 << 30, bytes_accessed=5 << 20, transcendentals=0),
        name="project",
    )(recv.reshape(8, 8, CH, 512), *weights)


def combine_kernel(keep, came, *outs):
    for index, out in enumerate(outs):
        block = jnp.bitwise_xor(column_index(), index)
        rows = pl.ds(pl.multiple_of(block * 64, 64), 64)
        out[...] = (keep[rows, :] + came[rows, :].astype(F32)).astype(BF)


def combine(keep, came):
    whole = pl.BlockSpec(memory_space=pltpu.VMEM)
    return pl.pallas_call(
        combine_kernel,
        out_shape=(jax.ShapeDtypeStruct((64, 1024), BF),) * 4,
        in_specs=[whole, whole],
        out_specs=(whole,) * 4,
        cost_estimate=pl.CostEstimate(flops=1 << 18, bytes_accessed=2 << 20, transcendentals=0),
        name="combine",
    )(keep, came)


def assemble_kernel(*refs):
    out = refs[-1]
    for index, piece in enumerate(refs[:-1]):
        block = jnp.bitwise_xor(column_index(), index)
        out[:, pl.ds(pl.multiple_of(block * 1024, 1024), 1024)] = piece[...]


def assemble(pieces):
    whole = pl.BlockSpec(memory_space=pltpu.VMEM)
    return pl.pallas_call(
        assemble_kernel,
        out_shape=jax.ShapeDtypeStruct((64, 4096), BF),
        in_specs=[whole] * 4,
        out_specs=whole,
        cost_estimate=pl.CostEstimate(flops=0, bytes_accessed=1 << 20, transcendentals=0),
        name="assemble",
    )(*pieces)


def permuted(block, move):
    pairs = []
    for place in itertools.product(*[range(SIZES[axis]) for axis in AXES]):
        here = dict(zip(AXES, place))
        there = {**here, **move(here)}
        index = [0, 0]
        for axis in AXES:
            index = [index[0] * SIZES[axis] + here[axis], index[1] * SIZES[axis] + there[axis]]
        pairs.append(tuple(index))
    return lax.ppermute(block, AXES, pairs)


def body(token_ids, embed_table, in_weight, short_filter, long_filter, skip_gain, out_weight):
    held = lax.dynamic_slice(
        out_weight.reshape(8, 2 * CH, 4096),
        (0, lax.axis_index("core") * CH, column_index() * 1024),
        (8, CH, 1024),
    ).reshape(128, 1024)
    weights = [held]
    for index in range(1, 8):
        dx, dz = index // 2, index % 2
        weights.append(permuted(held, lambda d: {"x": d["x"] ^ dx, "zh": d["zh"] ^ dz}))
    payload = pack(long_filter, token_ids)
    recv = lax.all_to_all(payload, SEQ, 0, 0, tiled=True)
    table = vocab(embed_table, in_weight)
    chunks = convolve(recv, table, short_filter, skip_gain)
    recv = lax.all_to_all(chunks.reshape(64, CH, 512), ("y", "zl", "x", "zh"), 0, 0, tiled=True)
    keep, send = project(recv, weights)
    came = permuted(send, lambda d: {"core": 1 - d["core"]})
    pieces = list(combine(keep, came))
    for index in range(1, 4):
        pieces[index] = permuted(pieces[index], lambda d: {"y": d["y"] ^ (index // 2), "zl": d["zl"] ^ (index % 2)})
    return assemble(pieces)


def solution(mesh):
    fine = Mesh(mesh.devices.reshape(tuple(SIZES.values())), AXES)
    return jax.shard_map(
        body,
        mesh=fine,
        in_specs=(
            P(SEQ),
            P(),
            P(None, None, CHAN),
            P(None, None, CHAN),
            P(SEQ, CHAN),
            P(CHAN),
            P(CHAN, None),
        ),
        out_specs=P(AXES, None),
        check_vma=False,
    )
```

```python
import functools
import itertools

import jax
import jax.numpy as jnp
import ml_dtypes
import numpy as np
from jax import lax
from jax.experimental import pallas as pl
from jax.experimental.pallas import tpu as pltpu
from jax.sharding import Mesh
from jax.sharding import PartitionSpec as P


SIZES = {"y": 4, "zl": 2, "core": 2, "x": 4, "zh": 2}
AXES = tuple(SIZES)
SEQ, CHAN = ("y", "zl", "core"), ("x", "zh")

N1 = 128
HALF = 72
CH = 16
BF, F32 = jnp.bfloat16, jnp.float32


def split_np(array):
    high = array.astype(np.float32).astype(ml_dtypes.bfloat16)
    low = (array - high.astype(np.float64)).astype(np.float32).astype(ml_dtypes.bfloat16)
    return high, low


@functools.cache
def tables():
    full = 2 * 8192
    freq = np.arange(HALF)[:, None]
    valid = (freq <= N1 // 2).astype(np.float64)
    block = np.arange(64)[None, :]
    angle = 2 * np.pi * (freq * block % N1) / N1
    first = np.concatenate([np.cos(angle) * valid, -np.sin(angle) * valid], 0)
    high, low = split_np(first)
    zero = np.zeros_like(high)
    first_signal = np.concatenate([high, high, low, zero], 1)
    rank = np.arange(64)
    order = 4 * (rank % 16) + rank // 16
    first_filter = np.concatenate([high[:, order], low[:, order]], 1)
    lane = np.arange(128)[None, :]
    turn = 2 * np.pi * (freq * lane) / full
    twiddle = np.stack([np.cos(turn) * valid, -np.sin(turn) * valid]).astype(np.float32)
    pair = 2 * np.pi * (np.arange(128)[:, None] * lane % 128) / 128
    cosine, sine = np.cos(pair), np.sin(pair)
    second = np.concatenate(
        [np.concatenate([cosine, -sine], 1), np.concatenate([sine, cosine], 1)], 0
    )
    second = np.stack(split_np(second))
    weight = np.where((freq == 0) | (freq == N1 // 2), 1.0, 2.0) * valid / full
    last = np.concatenate([np.cos(angle) * weight, -np.sin(angle) * weight], 0).T
    high, low = split_np(last)
    last = np.concatenate([high, high, low, np.zeros((64, 80), high.dtype)], 1)
    return first_signal, first_filter, twiddle, second, last


def halves(value):
    high = value.astype(BF)
    return high, (value - high.astype(F32)).astype(BF)


def mm(left, right, dims=(((1,), (0,)), ((), ()))):
    return lax.dot_general(left, right, dims, preferred_element_type=F32)


def seq_index():
    return (lax.axis_index("y") * 2 + lax.axis_index("zl")) * 2 + lax.axis_index("core")


def column_index():
    return lax.rem(lax.axis_index("y"), 2) * 2 + lax.axis_index("zl")


def pack_kernel(filt, tokens, payload):
    payload[:, :, :512] = filt[...].T.astype(BF).reshape(16, CH, 512)
    high = jnp.right_shift(tokens[...], 4)
    low = jnp.bitwise_and(tokens[...], 15)
    gap = jnp.zeros((4, 128), F32)
    digits = jnp.concatenate([high.astype(F32), gap, low.astype(F32), gap], 0).astype(BF)
    payload[:, :, 512:] = jnp.broadcast_to(digits[None], (16, CH, 128))


def pack(long_filter, token_ids):
    whole = pl.BlockSpec(memory_space=pltpu.VMEM)
    return pl.pallas_call(
        pack_kernel,
        out_shape=jax.ShapeDtypeStruct((16, CH, 640), BF),
        in_specs=[whole, whole],
        out_specs=whole,
        cost_estimate=pl.CostEstimate(flops=1 << 18, bytes_accessed=1 << 20, transcendentals=0),
        compiler_params=pltpu.CompilerParams(vmem_limit_bytes=6 << 20),
        name="pack",
    )(long_filter, token_ids.reshape(4, 128))


def vocab_kernel(embed, weight, table, acc):
    step = pl.program_id(0)
    wide = jnp.concatenate([weight[0], weight[1], weight[2]], 1)
    part = mm(embed[...], wide)

    @pl.when(step == 0)
    def _():
        acc[...] = part

    @pl.when(step > 0)
    def _():
        acc[...] += part

    @pl.when(step == pl.num_programs(0) - 1)
    def _():
        lane = lax.broadcasted_iota(jnp.int32, (CH, 128), 1)
        row = lax.broadcasted_iota(jnp.int32, (CH, 128), 0)
        pick = (lane == row + CH * lax.rem(seq_index(), 8)).astype(F32).astype(BF)
        for branch in range(3):
            rows = acc[:, branch * 128 : (branch + 1) * 128].astype(BF)
            table[branch * CH : (branch + 1) * CH, :] = mm(pick, rows, (((1,), (1,)), ((), ())))


def vocab(embed_table, in_weight):
    steps = 8
    depth = in_weight.shape[0] // steps
    return pl.pallas_call(
        vocab_kernel,
        out_shape=jax.ShapeDtypeStruct((3 * CH, 512), F32),
        grid_spec=pltpu.PrefetchScalarGridSpec(
            num_scalar_prefetch=0,
            grid=(steps,),
            in_specs=[
                pl.BlockSpec((512, depth), lambda i: (0, i)),
                pl.BlockSpec((3, depth, 128), lambda i: (0, i, lax.div(seq_index(), 8))),
            ],
            out_specs=pl.BlockSpec((3 * CH, 512), lambda i: (0, 0)),
            scratch_shapes=[pltpu.VMEM((512, 384), F32)],
        ),
        compiler_params=pltpu.CompilerParams(
            dimension_semantics=("arbitrary",), vmem_limit_bytes=61 << 20
        ),
        cost_estimate=pl.CostEstimate(flops=2 * 512 * 4096 * 384, bytes_accessed=8 << 20, transcendentals=0),
        name="vocab",
    )(embed_table, in_weight.transpose(1, 0, 2))


def convolve_kernel(
    recv, table, short, direct, first_signal, first_filter, twiddle, second, last,
    out, taps, token, gated, other, shaped, spec_high, spec_low, lags,
):
    seq, core = seq_index(), lax.axis_index("core")
    lane = lax.broadcasted_iota(jnp.int32, (CH, 256), 1)
    row = lax.broadcasted_iota(jnp.int32, (CH, 256), 0)
    mine = lane == row + CH * seq
    for index in range(10):
        wide = short[index // 3, index % 3 : index % 3 + 1, :] if index < 9 else direct[...]
        column = jnp.sum(jnp.where(mine, wide, 0.0), axis=1, keepdims=True)
        taps[index * CH : (index + 1) * CH, :] = jnp.broadcast_to(column, (CH, 128))

    for source in range(16):
        digits = recv[source, :, 512:].astype(F32)
        token[source * 8 : source * 8 + 8, :] = (digits[:8] * 16.0 + digits[8:]).astype(jnp.int32)
        for q in range(4):
            rows = slice(q * 256 + source * CH, q * 256 + (source + 1) * CH)
            lags[rows, :] = recv[source, :, q * 128 : (q + 1) * 128].astype(F32)

    position = lax.broadcasted_iota(jnp.int32, (3 * CH, 128), 1)

    def select(source, carried):
        before_one, before_two = carried
        for quarter in range(4):
            ids = jnp.broadcast_to(token[pl.ds(source * 8 + quarter, 1), :], (3 * CH, 128))
            place = jnp.bitwise_and(ids, 127)
            bank = jnp.right_shift(ids, 7)
            value = None
            for index in range(4):
                found = jnp.take_along_axis(
                    table[:, index * 128 : (index + 1) * 128], place, axis=1, mode="promise_in_bounds"
                )
                value = found if index == 0 else jnp.where(bank == index, found, value)
            one = pltpu.roll(value, 1, 1)
            two = pltpu.roll(value, 2, 1)
            lag_one = jnp.where(position < 1, before_one, one)
            lag_two = jnp.where(position < 2, before_two, two)
            before_one, before_two = one, two
            filtered = taps[: 3 * CH, :] * value
            filtered = filtered + taps[3 * CH : 6 * CH, :] * lag_one
            filtered = filtered + taps[6 * CH : 9 * CH, :] * lag_two
            rows = pl.ds(pl.multiple_of((source * 4 + quarter) * CH, CH), CH)
            gated[rows, :] = filtered[:CH] * filtered[2 * CH :]
            other[rows, :] = filtered[CH : 2 * CH]
        return before_one, before_two

    nothing = jnp.zeros((3 * CH, 128), F32)
    lax.fori_loop(0, 16, select, (nothing, nothing))

    cos_turn, sin_turn = twiddle[0], twiddle[1]
    rows_all = CH * HALF

    def turned(stage, sign):
        real, imag = stage[:HALF], stage[HALF:]
        return jnp.concatenate(
            [real * cos_turn - sign * imag * sin_turn, sign * real * sin_turn + imag * cos_turn], 1
        )

    for pair in range(CH // 2):
        signal = jnp.concatenate(
            [gated[pl.ds(2 * pair + i, 64, stride=CH), :] for i in range(2)], 1
        )
        high, low = halves(signal)
        stage = mm(first_signal[...], jnp.concatenate([high, low, high, high], 0))
        spectrum = jnp.concatenate([turned(stage[:, :128], 1), turned(stage[:, 128:], 1)], 0)
        at = slice(pair * 2 * HALF, (pair + 1) * 2 * HALF)
        spec_high[at, :], spec_low[at, :] = halves(spectrum)

        kernel = jnp.concatenate(
            [lags[pl.ds(2 * pair + i, 64, stride=CH), :] for i in range(2)], 1
        ).astype(BF)
        stage = mm(first_filter[...], jnp.concatenate([kernel, kernel], 0))
        spectrum = jnp.concatenate([turned(stage[:, :128], 1), turned(stage[:, 128:], 1)], 0)
        at = slice(rows_all + pair * 2 * HALF, rows_all + (pair + 1) * 2 * HALF)
        spec_high[at, :], spec_low[at, :] = halves(spectrum)

    def transform(at, dims):
        high, low = spec_high[at, :], spec_low[at, :]
        return mm(high, second[0], dims) + (mm(low, second[0], dims) + mm(high, second[1], dims))

    straight, flipped = (((1,), (0,)), ((), ())), (((1,), (1,)), ((), ()))
    for pair in range(CH // 2):
        at = slice(pair * 2 * HALF, (pair + 1) * 2 * HALF)
        left = transform(at, straight)
        right = transform(slice(rows_all + at.start, rows_all + at.stop), straight)
        left_real, left_imag, right_real, right_imag = left[:, :128], left[:, 128:], right[:, :128], right[:, 128:]
        product = jnp.concatenate(
            [left_real * right_real - left_imag * right_imag, left_real * right_imag + left_imag * right_real], 1
        )
        spec_high[at, :], spec_low[at, :] = halves(product)

    for pair in range(CH // 2):
        at = slice(pair * 2 * HALF, (pair + 1) * 2 * HALF)
        back = transform(at, flipped)
        columns = []
        for i in range(2):
            part = back[i * HALF : (i + 1) * HALF]
            real, imag = part[:, :128], part[:, 128:]
            columns.append(
                jnp.concatenate([real * cos_turn + imag * sin_turn, imag * cos_turn - real * sin_turn], 0)
            )
        high, low = halves(jnp.concatenate(columns, 1))
        result = mm(last[...], jnp.concatenate([high, low, high, high[:80]], 0))
        for i in range(2):
            shaped[pl.ds(2 * pair + i, 64, stride=CH), :] = result[:, i * 128 : (i + 1) * 128]

    skip = taps[9 * CH :, :]
    low_half = lax.broadcasted_iota(jnp.int32, (CH, 128), 1) < 64
    for a, top, core_to, h in itertools.product(range(2), range(2), range(2), range(4)):
        done = []
        for zl in range(2):
            shard = 8 * a + top * 4 + zl * 2 + core_to
            rows = slice((4 * shard + h) * CH, (4 * shard + h + 1) * CH)
            done.append(other[rows, :] * (shaped[rows, :] + skip * gated[rows, :]))
        first, then = done
        even = jnp.where(low_half, first, pltpu.roll(then, 64, 1)).astype(BF)
        odd = jnp.where(low_half, pltpu.roll(first, 64, 1), then).astype(BF)
        half = jnp.bitwise_xor(core, core_to) if core_to else core
        columns = pl.ds(pl.multiple_of(half * 256 + top * 128, 128), 128)
        for to_y, to_z in itertools.product(range(2), range(2)):
            out[a, to_y, to_z, 2 * h, :, columns] = even
            out[a, to_y, to_z, 2 * h + 1, :, columns] = odd


def convolve(recv, table, short_filter, skip_gain):
    consts = [jnp.asarray(c) for c in tables()]
    whole = pl.BlockSpec(memory_space=pltpu.VMEM)
    positions = 8192
    return pl.pallas_call(
        convolve_kernel,
        out_shape=jax.ShapeDtypeStruct((2, 2, 2, 8, CH, 512), BF),
        in_specs=[whole] * 9,
        out_specs=whole,
        scratch_shapes=[
            pltpu.VMEM((10 * CH, 128), F32),
            pltpu.VMEM((128, 128), jnp.int32),
            pltpu.VMEM((positions // 128 * CH, 128), F32),
            pltpu.VMEM((positions // 128 * CH, 128), F32),
            pltpu.VMEM((positions // 128 * CH, 128), F32),
            pltpu.VMEM((2 * CH * HALF, 256), BF),
            pltpu.VMEM((2 * CH * HALF, 256), BF),
            pltpu.VMEM((64 * CH, 128), F32),
        ],
        cost_estimate=pl.CostEstimate(flops=4 << 30, bytes_accessed=4 << 20, transcendentals=0),
        compiler_params=pltpu.CompilerParams(vmem_limit_bytes=20 << 20),
        name="convolve",
    )(recv, table, short_filter, skip_gain[None, :], *consts)


def project_kernel(recv, *refs):
    weights, keep, send = refs[:4], refs[4], refs[5]
    chan = lax.axis_index("x") * 2 + lax.axis_index("zh")
    total = None
    for index in range(4):
        lhs = jnp.concatenate(
            [recv[:, jnp.bitwise_xor(chan, 2 * index + i)].reshape(128, 512) for i in range(2)], 0
        )
        part = mm(lhs, weights[index][...], (((0,), (0,)), ((), ())))
        total = part if total is None else total + part
    keep[...] = total[:256]
    send[...] = total[256:].astype(BF)


def project(recv, weights):
    whole = pl.BlockSpec(memory_space=pltpu.VMEM)
    return pl.pallas_call(
        project_kernel,
        out_shape=(jax.ShapeDtypeStruct((256, 1024), F32), jax.ShapeDtypeStruct((256, 1024), BF)),
        in_specs=[whole] * 5,
        out_specs=(whole, whole),
        cost_estimate=pl.CostEstimate(flops=1 << 30, bytes_accessed=5 << 20, transcendentals=0),
        compiler_params=pltpu.CompilerParams(vmem_limit_bytes=20 << 20),
        name="project",
    )(recv.reshape(8, 8, CH, 512), *weights)


def combine_kernel(keep, came, *outs):
    for index, out in enumerate(outs):
        block = jnp.bitwise_xor(column_index(), index)
        rows = pl.ds(pl.multiple_of(block * 64, 64), 64)
        out[...] = (keep[rows, :] + came[rows, :].astype(F32)).astype(BF)


def combine(keep, came):
    whole = pl.BlockSpec(memory_space=pltpu.VMEM)
    return pl.pallas_call(
        combine_kernel,
        out_shape=(jax.ShapeDtypeStruct((64, 1024), BF),) * 4,
        in_specs=[whole, whole],
        out_specs=(whole,) * 4,
        cost_estimate=pl.CostEstimate(flops=1 << 18, bytes_accessed=2 << 20, transcendentals=0),
        compiler_params=pltpu.CompilerParams(vmem_limit_bytes=6 << 20),
        name="combine",
    )(keep, came)


def assemble_kernel(*refs):
    out = refs[-1]
    for index, piece in enumerate(refs[:-1]):
        block = jnp.bitwise_xor(column_index(), index)
        out[:, pl.ds(pl.multiple_of(block * 1024, 1024), 1024)] = piece[...]


def assemble(pieces):
    whole = pl.BlockSpec(memory_space=pltpu.VMEM)
    return pl.pallas_call(
        assemble_kernel,
        out_shape=jax.ShapeDtypeStruct((64, 4096), BF),
        in_specs=[whole] * 4,
        out_specs=whole,
        cost_estimate=pl.CostEstimate(flops=0, bytes_accessed=1 << 20, transcendentals=0),
        compiler_params=pltpu.CompilerParams(vmem_limit_bytes=4 << 20),
        name="assemble",
    )(*pieces)


def permuted(block, move):
    pairs = []
    for place in itertools.product(*[range(SIZES[axis]) for axis in AXES]):
        here = dict(zip(AXES, place))
        there = {**here, **move(here)}
        index = [0, 0]
        for axis in AXES:
            index = [index[0] * SIZES[axis] + here[axis], index[1] * SIZES[axis] + there[axis]]
        pairs.append(tuple(index))
    return lax.ppermute(block, AXES, pairs)


def body(token_ids, embed_table, in_weight, short_filter, long_filter, skip_gain, out_weight):
    held = lax.dynamic_slice(
        out_weight.reshape(8, 2 * CH, 4096),
        (0, lax.axis_index("core") * CH, column_index() * 1024),
        (8, CH, 1024),
    ).reshape(128, 1024)
    across = permuted(held, lambda d: {"zh": d["zh"] ^ 1})
    both = jnp.concatenate([held, across], 0)
    weights = [both]
    for index in range(1, 4):
        weights.append(permuted(both, lambda d: {"x": d["x"] ^ index}))
    payload = pack(long_filter, token_ids)
    recv = lax.all_to_all(payload, SEQ, 0, 0, tiled=True)
    table = vocab(embed_table, in_weight)
    chunks = convolve(recv, table, short_filter, skip_gain)
    recv = lax.all_to_all(chunks.reshape(64, CH, 512), ("y", "zl", "x", "zh"), 0, 0, tiled=True)
    keep, send = project(recv, weights)
    came = permuted(send, lambda d: {"core": 1 - d["core"]})
    pieces = list(combine(keep, came))
    for index in range(1, 4):
        pieces[index] = permuted(
            pieces[index], lambda d: {"y": d["y"] ^ (index // 2), "zl": d["zl"] ^ (index % 2)}
        )
    return assemble(pieces)


def solution(mesh):
    fine = Mesh(mesh.devices.reshape(tuple(SIZES.values())), AXES)
    return jax.shard_map(
        body,
        mesh=fine,
        in_specs=(
            P(SEQ),
            P(),
            P(None, None, CHAN),
            P(None, None, CHAN),
            P(SEQ, CHAN),
            P(CHAN),
            P(CHAN, None),
        ),
        out_specs=P(AXES, None),
        check_vma=False,
    )
```

```python
import functools
import itertools

import jax
import jax.numpy as jnp
import ml_dtypes
import numpy as np
from jax import lax
from jax.experimental import pallas as pl
from jax.experimental.pallas import tpu as pltpu
from jax.sharding import Mesh
from jax.sharding import PartitionSpec as P


SIZES = {"y": 4, "zl": 2, "core": 2, "x": 4, "zh": 2}
AXES = tuple(SIZES)
SEQ, CHAN = ("y", "zl", "core"), ("x", "zh")

N1 = 128
HALF = 72
CH = 16
BF, F32 = jnp.bfloat16, jnp.float32


def split_np(array):
    high = array.astype(np.float32).astype(ml_dtypes.bfloat16)
    low = (array - high.astype(np.float64)).astype(np.float32).astype(ml_dtypes.bfloat16)
    return high, low


@functools.cache
def tables():
    full = 2 * 8192
    freq = np.arange(HALF)[:, None]
    valid = (freq <= N1 // 2).astype(np.float64)
    block = np.arange(64)[None, :]
    angle = 2 * np.pi * (freq * block % N1) / N1
    first = np.concatenate([np.cos(angle) * valid, -np.sin(angle) * valid], 0)
    high, low = split_np(first)
    zero = np.zeros_like(high)
    first_signal = np.concatenate([high, high, low, zero], 1)
    rank = np.arange(64)
    order = 4 * (rank % 16) + rank // 16
    first_filter = np.concatenate([high[:, order], low[:, order]], 1)
    lane = np.arange(128)[None, :]
    turn = 2 * np.pi * (freq * lane) / full
    twiddle = np.stack([np.cos(turn) * valid, -np.sin(turn) * valid]).astype(np.float32)
    pair = 2 * np.pi * (np.arange(128)[:, None] * lane % 128) / 128
    cosine, sine = np.cos(pair), np.sin(pair)
    second = np.concatenate(
        [np.concatenate([cosine, -sine], 1), np.concatenate([sine, cosine], 1)], 0
    )
    second = np.stack(split_np(second))
    weight = np.where((freq == 0) | (freq == N1 // 2), 1.0, 2.0) * valid / full
    last = np.concatenate([np.cos(angle) * weight, -np.sin(angle) * weight], 0).T
    high, low = split_np(last)
    last = np.concatenate([high, high, low, np.zeros((64, 80), high.dtype)], 1)
    return first_signal, first_filter, twiddle, second, last


def halves(value):
    high = value.astype(BF)
    return high, (value - high.astype(F32)).astype(BF)


def mm(left, right, dims=(((1,), (0,)), ((), ()))):
    return lax.dot_general(left, right, dims, preferred_element_type=F32)


def in_hbm(array):
    return pltpu.with_memory_space_constraint(array, pltpu.HBM)


def seq_index():
    return (lax.axis_index("y") * 2 + lax.axis_index("zl")) * 2 + lax.axis_index("core")


def column_index():
    return lax.rem(lax.axis_index("y"), 2) * 2 + lax.axis_index("zl")


def pack_kernel(filt_hbm, tokens_hbm, payload, filt, tokens, sems):
    parts = 4
    rows = 512 // parts
    copies = [
        pltpu.make_async_copy(filt_hbm.at[i * rows : (i + 1) * rows], filt.at[i * rows : (i + 1) * rows], sems.at[i])
        for i in range(parts)
    ]
    copies.append(pltpu.make_async_copy(tokens_hbm, tokens, sems.at[parts]))
    for copy in copies:
        copy.start()
    copies[parts].wait()
    high = jnp.right_shift(tokens[...], 4)
    low = jnp.bitwise_and(tokens[...], 15)
    gap = jnp.zeros((4, 128), F32)
    digits = jnp.concatenate([high.astype(F32), gap, low.astype(F32), gap], 0).astype(BF)
    payload[:, :, 512:] = jnp.broadcast_to(digits[None], (16, CH, 128))
    for i in range(parts):
        copies[i].wait()
        at = slice(i * rows, (i + 1) * rows)
        payload[:, :, at] = filt[at, :].T.astype(BF).reshape(16, CH, rows)


def pack(long_filter, token_ids):
    hbm = pl.BlockSpec(memory_space=pltpu.HBM)
    return pl.pallas_call(
        pack_kernel,
        out_shape=jax.ShapeDtypeStruct((16, CH, 640), BF),
        in_specs=[hbm, hbm],
        out_specs=pl.BlockSpec(memory_space=pltpu.VMEM),
        scratch_shapes=[
            pltpu.VMEM((512, 256), F32),
            pltpu.VMEM((4, 128), jnp.int32),
            pltpu.SemaphoreType.DMA((5,)),
        ],
        cost_estimate=pl.CostEstimate(flops=1 << 18, bytes_accessed=1 << 20, transcendentals=0),
        compiler_params=pltpu.CompilerParams(vmem_limit_bytes=6 << 20),
        name="pack",
    )(in_hbm(long_filter), in_hbm(token_ids.reshape(4, 128)))


STEPS = 4
GROUP = 8
UNROLL = 16


def vocab_kernel(embed_hbm, weight_hbm, table, embed, weight, sems):
    depth = 4096 // STEPS
    lanes = pl.ds(pl.multiple_of(lax.div(seq_index(), 8) * 128, 128), 128)
    copies = []
    for step in range(STEPS):
        at = slice(step * depth, (step + 1) * depth)
        pair = [pltpu.make_async_copy(embed_hbm.at[:, at], embed.at[:, at], sems.at[4 * step + 3])]
        for branch in range(3):
            pair.append(
                pltpu.make_async_copy(
                    weight_hbm.at[branch, at, lanes],
                    weight.at[at, branch * 128 : (branch + 1) * 128],
                    sems.at[4 * step + branch],
                )
            )
        copies.append(pair)
    for pair in copies:
        for copy in pair:
            copy.start()
    total = None
    for step, pair in enumerate(copies):
        for copy in pair:
            copy.wait()
        at = slice(step * depth, (step + 1) * depth)
        part = mm(embed[:, at], weight[at, :])
        total = part if total is None else total + part
    lane = lax.broadcasted_iota(jnp.int32, (CH, 128), 1)
    row = lax.broadcasted_iota(jnp.int32, (CH, 128), 0)
    pick = (lane == row + CH * lax.rem(seq_index(), 8)).astype(F32).astype(BF)
    for branch in range(3):
        rows = total[:, branch * 128 : (branch + 1) * 128].astype(BF)
        table[branch * CH : (branch + 1) * CH, :] = mm(pick, rows, (((1,), (1,)), ((), ())))


def vocab(embed_table, in_weight):
    hbm = pl.BlockSpec(memory_space=pltpu.HBM)
    return pl.pallas_call(
        vocab_kernel,
        out_shape=jax.ShapeDtypeStruct((3 * CH, 512), F32),
        in_specs=[hbm, hbm],
        out_specs=pl.BlockSpec(memory_space=pltpu.VMEM),
        scratch_shapes=[
            pltpu.VMEM((512, 4096), BF),
            pltpu.VMEM((4096, 384), BF),
            pltpu.SemaphoreType.DMA((4 * STEPS,)),
        ],
        compiler_params=pltpu.CompilerParams(vmem_limit_bytes=16 << 20),
        cost_estimate=pl.CostEstimate(flops=2 * 512 * 4096 * 384, bytes_accessed=8 << 20, transcendentals=0),
        name="vocab",
    )(in_hbm(embed_table), in_hbm(in_weight.transpose(1, 0, 2)))


def convolve_kernel(
    recv, table, *refs,
):
    sources, (out, taps, token, gated, other, shaped, spec_high, spec_low, lags) = refs[:7], refs[7:16]
    short, direct, first_signal, first_filter, twiddle, second, last = held = refs[16:23]
    copies = [
        pltpu.make_async_copy(source, target, refs[23].at[index])
        for index, (source, target) in enumerate(zip(sources, held))
    ]
    for copy in copies:
        copy.start()
    copies[0].wait()
    copies[1].wait()
    seq, core = seq_index(), lax.axis_index("core")
    lane = lax.broadcasted_iota(jnp.int32, (CH, 256), 1)
    row = lax.broadcasted_iota(jnp.int32, (CH, 256), 0)
    mine = lane == row + CH * seq
    for index in range(10):
        wide = short[index // 3, index % 3 : index % 3 + 1, :] if index < 9 else direct[...]
        column = jnp.sum(jnp.where(mine, wide, 0.0), axis=1, keepdims=True)
        taps[index * CH : (index + 1) * CH, :] = jnp.broadcast_to(column, (CH, 128))

    for source in range(16):
        digits = recv[source, :, 512:].astype(F32)
        token[source * 8 : source * 8 + 8, :] = (digits[:8] * 16.0 + digits[8:]).astype(jnp.int32)
        for q in range(4):
            rows = slice(q * 256 + source * CH, q * 256 + (source + 1) * CH)
            lags[rows, :] = recv[source, :, q * 128 : (q + 1) * 128].astype(F32)

    banks = jnp.concatenate([table[:, i * 128 : (i + 1) * 128] for i in range(4)], 0).astype(BF)
    line = lax.broadcasted_iota(jnp.int32, (256, 256), 0)
    lane = lax.broadcasted_iota(jnp.int32, (256, 256), 1)
    shift = (line == jnp.where(lane < 128, lane + 127, lane - 2)).astype(F32).astype(BF)
    entry = lax.broadcasted_iota(jnp.int32, (128, 128), 0)

    def select(source, before):
        rows = [token[pl.ds(source * 8 + q, 1), :] for q in range(4)]
        chosen = [(entry == jnp.bitwise_and(row, 127)).astype(F32).astype(BF) for row in rows]
        found = mm(banks, jnp.concatenate(chosen, 1))
        bank = jnp.right_shift(jnp.concatenate(rows, 1), 7)
        value = found[: 3 * CH]
        for i in range(1, 4):
            value = jnp.where(bank == i, found[i * 3 * CH : (i + 1) * 3 * CH], value)
        narrow = value.astype(BF)
        blocks = [before] + [narrow[:, q * 128 : (q + 1) * 128] for q in range(4)]
        pairs = [jnp.concatenate([blocks[q], blocks[q + 1]], 1) for q in range(4)]
        lagged = mm(jnp.concatenate(pairs, 0), shift)
        for q in range(4):
            lag = lagged[q * 3 * CH : (q + 1) * 3 * CH]
            filtered = taps[: 3 * CH, :] * value[:, q * 128 : (q + 1) * 128]
            filtered = filtered + taps[3 * CH : 6 * CH, :] * lag[:, :128]
            filtered = filtered + taps[6 * CH : 9 * CH, :] * lag[:, 128:]
            at = pl.ds(pl.multiple_of((source * 4 + q) * CH, CH), CH)
            gated[at, :] = filtered[:CH] * filtered[2 * CH :]
            other[at, :] = filtered[CH : 2 * CH]
        return blocks[4]

    lax.fori_loop(0, 16, select, jnp.zeros((3 * CH, 128), BF), unroll=UNROLL)

    for copy in copies[2:]:
        copy.wait()
    cos_turn, sin_turn = twiddle[0], twiddle[1]
    rows_all = CH * HALF

    def turned(stage, sign):
        real, imag = stage[:HALF], stage[HALF:]
        return jnp.concatenate(
            [real * cos_turn - sign * imag * sin_turn, sign * real * sin_turn + imag * cos_turn], 1
        )

    for pair in range(CH // 2):
        signal = jnp.concatenate(
            [gated[pl.ds(2 * pair + i, 64, stride=CH), :] for i in range(2)], 1
        )
        high, low = halves(signal)
        stage = mm(first_signal[...], jnp.concatenate([high, low, high, high], 0))
        spectrum = jnp.concatenate([turned(stage[:, :128], 1), turned(stage[:, 128:], 1)], 0)
        at = slice(pair * 2 * HALF, (pair + 1) * 2 * HALF)
        spec_high[at, :], spec_low[at, :] = halves(spectrum)

        kernel = jnp.concatenate(
            [lags[pl.ds(2 * pair + i, 64, stride=CH), :] for i in range(2)], 1
        ).astype(BF)
        stage = mm(first_filter[...], jnp.concatenate([kernel, kernel], 0))
        spectrum = jnp.concatenate([turned(stage[:, :128], 1), turned(stage[:, 128:], 1)], 0)
        at = slice(rows_all + pair * 2 * HALF, rows_all + (pair + 1) * 2 * HALF)
        spec_high[at, :], spec_low[at, :] = halves(spectrum)

    def transform(at, dims):
        high, low = spec_high[at, :], spec_low[at, :]
        return mm(high, second[0], dims) + (mm(low, second[0], dims) + mm(high, second[1], dims))

    straight, flipped = (((1,), (0,)), ((), ())), (((1,), (1,)), ((), ()))
    span = 2 * HALF
    for start in range(0, CH // 2, GROUP):
        at = slice(start * span, (start + GROUP) * span)
        left = transform(at, straight)
        right = transform(slice(rows_all + at.start, rows_all + at.stop), straight)
        left_real, left_imag, right_real, right_imag = left[:, :128], left[:, 128:], right[:, :128], right[:, 128:]
        product = jnp.concatenate(
            [left_real * right_real - left_imag * right_imag, left_real * right_imag + left_imag * right_real], 1
        )
        spec_high[at, :], spec_low[at, :] = halves(product)

    for start in range(0, CH // 2, GROUP):
        backs = transform(slice(start * span, (start + GROUP) * span), flipped)
        for pair in range(start, start + GROUP):
            columns = []
            for i in range(2):
                top = ((pair - start) * 2 + i) * HALF
                real, imag = backs[top : top + HALF, :128], backs[top : top + HALF, 128:]
                columns.append(
                    jnp.concatenate([real * cos_turn + imag * sin_turn, imag * cos_turn - real * sin_turn], 0)
                )
            high, low = halves(jnp.concatenate(columns, 1))
            result = mm(last[...], jnp.concatenate([high, low, high, high[:80]], 0))
            for i in range(2):
                shaped[pl.ds(2 * pair + i, 64, stride=CH), :] = result[:, i * 128 : (i + 1) * 128]

    skip = taps[9 * CH :, :]
    low_half = lax.broadcasted_iota(jnp.int32, (CH, 128), 1) < 64
    for a, top, core_to, h in itertools.product(range(2), range(2), range(2), range(4)):
        done = []
        for zl in range(2):
            shard = 8 * a + top * 4 + zl * 2 + core_to
            rows = slice((4 * shard + h) * CH, (4 * shard + h + 1) * CH)
            done.append(other[rows, :] * (shaped[rows, :] + skip * gated[rows, :]))
        first, then = done
        even = jnp.where(low_half, first, pltpu.roll(then, 64, 1)).astype(BF)
        odd = jnp.where(low_half, pltpu.roll(first, 64, 1), then).astype(BF)
        half = jnp.bitwise_xor(core, core_to) if core_to else core
        columns = pl.ds(pl.multiple_of(half * 256 + top * 128, 128), 128)
        for to_y, to_z in itertools.product(range(2), range(2)):
            out[a, to_y, to_z, 2 * h, :, columns] = even
            out[a, to_y, to_z, 2 * h + 1, :, columns] = odd


def convolve(recv, table, short_filter, skip_gain):
    consts = [jnp.asarray(c) for c in tables()]
    whole, hbm = pl.BlockSpec(memory_space=pltpu.VMEM), pl.BlockSpec(memory_space=pltpu.HBM)
    positions = 8192
    fetched = [short_filter, skip_gain[None, :], *consts]
    return pl.pallas_call(
        convolve_kernel,
        out_shape=jax.ShapeDtypeStruct((2, 2, 2, 8, CH, 512), BF),
        in_specs=[whole] * 2 + [hbm] * 7,
        out_specs=whole,
        scratch_shapes=[
            pltpu.VMEM((10 * CH, 128), F32),
            pltpu.VMEM((128, 128), jnp.int32),
            pltpu.VMEM((positions // 128 * CH, 128), F32),
            pltpu.VMEM((positions // 128 * CH, 128), F32),
            pltpu.VMEM((positions // 128 * CH, 128), F32),
            pltpu.VMEM((2 * CH * HALF, 256), BF),
            pltpu.VMEM((2 * CH * HALF, 256), BF),
            pltpu.VMEM((64 * CH, 128), F32),
            *[pltpu.VMEM(array.shape, array.dtype) for array in fetched],
            pltpu.SemaphoreType.DMA((len(fetched),)),
        ],
        cost_estimate=pl.CostEstimate(flops=4 << 30, bytes_accessed=4 << 20, transcendentals=0),
        compiler_params=pltpu.CompilerParams(vmem_limit_bytes=20 << 20),
        name="convolve",
    )(recv, table, *[in_hbm(array) for array in fetched])


def project_kernel(recv, *refs):
    weights, keep, send = refs[:4], refs[4], refs[5]
    chan = lax.axis_index("x") * 2 + lax.axis_index("zh")
    total = None
    for index in range(4):
        lhs = jnp.concatenate(
            [recv[:, jnp.bitwise_xor(chan, 2 * index + i)].reshape(128, 512) for i in range(2)], 0
        )
        part = mm(lhs, weights[index][...], (((0,), (0,)), ((), ())))
        total = part if total is None else total + part
    keep[...] = total[:256]
    send[...] = total[256:].astype(BF)


def project(recv, weights):
    whole = pl.BlockSpec(memory_space=pltpu.VMEM)
    return pl.pallas_call(
        project_kernel,
        out_shape=(jax.ShapeDtypeStruct((256, 1024), F32), jax.ShapeDtypeStruct((256, 1024), BF)),
        in_specs=[whole] * 5,
        out_specs=(whole, whole),
        cost_estimate=pl.CostEstimate(flops=1 << 30, bytes_accessed=5 << 20, transcendentals=0),
        compiler_params=pltpu.CompilerParams(vmem_limit_bytes=20 << 20),
        name="project",
    )(recv.reshape(8, 8, CH, 512), *weights)


def combine_kernel(keep, came, *outs):
    for index, out in enumerate(outs):
        block = jnp.bitwise_xor(column_index(), index)
        rows = pl.ds(pl.multiple_of(block * 64, 64), 64)
        out[...] = (keep[rows, :] + came[rows, :].astype(F32)).astype(BF)


def combine(keep, came):
    whole = pl.BlockSpec(memory_space=pltpu.VMEM)
    return pl.pallas_call(
        combine_kernel,
        out_shape=(jax.ShapeDtypeStruct((64, 1024), BF),) * 4,
        in_specs=[whole, whole],
        out_specs=(whole,) * 4,
        cost_estimate=pl.CostEstimate(flops=1 << 18, bytes_accessed=2 << 20, transcendentals=0),
        compiler_params=pltpu.CompilerParams(vmem_limit_bytes=6 << 20),
        name="combine",
    )(keep, came)


def assemble_kernel(*refs):
    out = refs[-1]
    for index, piece in enumerate(refs[:-1]):
        block = jnp.bitwise_xor(column_index(), index)
        out[:, pl.ds(pl.multiple_of(block * 1024, 1024), 1024)] = piece[...]


def assemble(pieces):
    whole = pl.BlockSpec(memory_space=pltpu.VMEM)
    return pl.pallas_call(
        assemble_kernel,
        out_shape=jax.ShapeDtypeStruct((64, 4096), BF),
        in_specs=[whole] * 4,
        out_specs=whole,
        cost_estimate=pl.CostEstimate(flops=0, bytes_accessed=1 << 20, transcendentals=0),
        compiler_params=pltpu.CompilerParams(vmem_limit_bytes=4 << 20),
        name="assemble",
    )(*pieces)


def permuted(block, move):
    pairs = []
    for place in itertools.product(*[range(SIZES[axis]) for axis in AXES]):
        here = dict(zip(AXES, place))
        there = {**here, **move(here)}
        index = [0, 0]
        for axis in AXES:
            index = [index[0] * SIZES[axis] + here[axis], index[1] * SIZES[axis] + there[axis]]
        pairs.append(tuple(index))
    return lax.ppermute(block, AXES, pairs)


def body(token_ids, embed_table, in_weight, short_filter, long_filter, skip_gain, out_weight):
    held = lax.dynamic_slice(
        out_weight.reshape(8, 2 * CH, 4096),
        (0, lax.axis_index("core") * CH, column_index() * 1024),
        (8, CH, 1024),
    ).reshape(128, 1024)
    across = permuted(held, lambda d: {"zh": d["zh"] ^ 1})
    both = jnp.concatenate([held, across], 0)
    weights = [both]
    for index in range(1, 4):
        weights.append(permuted(both, lambda d: {"x": d["x"] ^ index}))
    payload = pack(long_filter, token_ids)
    recv = lax.all_to_all(payload, SEQ, 0, 0, tiled=True)
    table = vocab(embed_table, in_weight)
    chunks = convolve(recv, table, short_filter, skip_gain)
    recv = lax.all_to_all(chunks.reshape(64, CH, 512), ("y", "zl", "x", "zh"), 0, 0, tiled=True)
    keep, send = project(recv, weights)
    came = permuted(send, lambda d: {"core": 1 - d["core"]})
    pieces = list(combine(keep, came))
    for index in range(1, 4):
        pieces[index] = permuted(
            pieces[index], lambda d: {"y": d["y"] ^ (index // 2), "zl": d["zl"] ^ (index % 2)}
        )
    return assemble(pieces)


def solution(mesh):
    fine = Mesh(mesh.devices.reshape(tuple(SIZES.values())), AXES)
    return jax.shard_map(
        body,
        mesh=fine,
        in_specs=(
            P(SEQ),
            P(),
            P(None, None, CHAN),
            P(None, None, CHAN),
            P(SEQ, CHAN),
            P(CHAN),
            P(CHAN, None),
        ),
        out_specs=P(AXES, None),
        check_vma=False,
    )
```

```python
import functools
import itertools

import jax
import jax.numpy as jnp
import ml_dtypes
import numpy as np
from jax import lax
from jax.experimental import pallas as pl
from jax.experimental.pallas import tpu as pltpu
from jax.sharding import Mesh
from jax.sharding import PartitionSpec as P


SIZES = {"y": 4, "zl": 2, "core": 2, "x": 4, "zh": 2}
AXES = tuple(SIZES)
SEQ, CHAN = ("y", "zl", "core"), ("x", "zh")

N1 = 128
HALF = 72
CH = 16
BF, F32 = jnp.bfloat16, jnp.float32


def split_np(array):
    high = array.astype(np.float32).astype(ml_dtypes.bfloat16)
    low = (array - high.astype(np.float64)).astype(np.float32).astype(ml_dtypes.bfloat16)
    return high, low


@functools.cache
def tables():
    full = 2 * 8192
    freq = np.arange(HALF)[:, None]
    valid = (freq <= N1 // 2).astype(np.float64)
    block = np.arange(64)[None, :]
    angle = 2 * np.pi * (freq * block % N1) / N1
    first = np.concatenate([np.cos(angle) * valid, -np.sin(angle) * valid], 0)
    high, low = split_np(first)
    zero = np.zeros_like(high)
    first_signal = np.concatenate([high, high, low, zero], 1)
    rank = np.arange(64)
    order = 4 * (rank % 16) + rank // 16
    first_filter = np.concatenate([high[:, order], low[:, order]], 1)
    lane = np.arange(128)[None, :]
    turn = 2 * np.pi * (freq * lane) / full
    twiddle = np.stack([np.cos(turn) * valid, -np.sin(turn) * valid]).astype(np.float32)
    pair = 2 * np.pi * (np.arange(128)[:, None] * lane % 128) / 128
    cosine, sine = np.cos(pair), np.sin(pair)
    second = np.concatenate(
        [np.concatenate([cosine, -sine], 1), np.concatenate([sine, cosine], 1)], 0
    )
    second = np.stack(split_np(second))
    weight = np.where((freq == 0) | (freq == N1 // 2), 1.0, 2.0) * valid / full
    last = np.concatenate([np.cos(angle) * weight, -np.sin(angle) * weight], 0).T
    high, low = split_np(last)
    last = np.concatenate([high, high, low, np.zeros((64, 80), high.dtype)], 1)
    return first_signal, first_filter, twiddle, second, last


def halves(value):
    high = value.astype(BF)
    return high, (value - high.astype(F32)).astype(BF)


def mm(left, right, dims=(((1,), (0,)), ((), ()))):
    return lax.dot_general(left, right, dims, preferred_element_type=F32)


def in_hbm(array):
    return pltpu.with_memory_space_constraint(array, pltpu.HBM)


def seq_index():
    return (lax.axis_index("y") * 2 + lax.axis_index("zl")) * 2 + lax.axis_index("core")


def column_index():
    return lax.rem(lax.axis_index("y"), 2) * 2 + lax.axis_index("zl")


def pack_kernel(filt_hbm, tokens_hbm, weight_hbm, payload, held, filt, tokens, sems):
    parts = 4
    mine = weight_hbm.at[
        :,
        pl.ds(pl.multiple_of(lax.axis_index("core") * CH, CH), CH),
        pl.ds(pl.multiple_of(column_index() * 1024, 1024), 1024),
    ]
    rows = 512 // parts
    copies = [
        pltpu.make_async_copy(filt_hbm.at[i * rows : (i + 1) * rows], filt.at[i * rows : (i + 1) * rows], sems.at[i])
        for i in range(parts)
    ]
    copies.append(pltpu.make_async_copy(tokens_hbm, tokens, sems.at[parts]))
    copies.append(pltpu.make_async_copy(mine, held, sems.at[parts + 1]))
    for copy in copies:
        copy.start()
    copies[parts].wait()
    high = jnp.right_shift(tokens[...], 4)
    low = jnp.bitwise_and(tokens[...], 15)
    gap = jnp.zeros((4, 128), F32)
    digits = jnp.concatenate([high.astype(F32), gap, low.astype(F32), gap], 0).astype(BF)
    payload[:, :, 512:] = jnp.broadcast_to(digits[None], (16, CH, 128))
    for i in range(parts):
        copies[i].wait()
        at = slice(i * rows, (i + 1) * rows)
        payload[:, :, at] = filt[at, :].T.astype(BF).reshape(16, CH, rows)
    copies[parts + 1].wait()


def pack(long_filter, token_ids, out_weight):
    hbm, whole = pl.BlockSpec(memory_space=pltpu.HBM), pl.BlockSpec(memory_space=pltpu.VMEM)
    return pl.pallas_call(
        pack_kernel,
        out_shape=(
            jax.ShapeDtypeStruct((16, CH, 640), BF),
            jax.ShapeDtypeStruct((8, CH, 1024), BF),
        ),
        in_specs=[hbm] * 3,
        out_specs=(whole, whole),
        scratch_shapes=[
            pltpu.VMEM((512, 256), F32),
            pltpu.VMEM((4, 128), jnp.int32),
            pltpu.SemaphoreType.DMA((6,)),
        ],
        cost_estimate=pl.CostEstimate(flops=1 << 18, bytes_accessed=1 << 20, transcendentals=0),
        compiler_params=pltpu.CompilerParams(vmem_limit_bytes=6 << 20),
        name="pack",
    )(in_hbm(long_filter), in_hbm(token_ids.reshape(4, 128)), in_hbm(out_weight.reshape(8, 2 * CH, 4096)))


STEPS = 4
GROUP = 8
UNROLL = 16


def vocab_kernel(embed_hbm, weight_hbm, table, embed, weight, sems):
    depth = 4096 // STEPS
    lanes = pl.ds(pl.multiple_of(lax.div(seq_index(), 8) * 128, 128), 128)
    copies = []
    for step in range(STEPS):
        at = slice(step * depth, (step + 1) * depth)
        pair = [pltpu.make_async_copy(embed_hbm.at[:, at], embed.at[:, at], sems.at[4 * step + 3])]
        for branch in range(3):
            pair.append(
                pltpu.make_async_copy(
                    weight_hbm.at[branch, at, lanes],
                    weight.at[at, branch * 128 : (branch + 1) * 128],
                    sems.at[4 * step + branch],
                )
            )
        copies.append(pair)
    for pair in copies:
        for copy in pair:
            copy.start()
    total = None
    for step, pair in enumerate(copies):
        for copy in pair:
            copy.wait()
        at = slice(step * depth, (step + 1) * depth)
        part = mm(embed[:, at], weight[at, :])
        total = part if total is None else total + part
    lane = lax.broadcasted_iota(jnp.int32, (CH, 128), 1)
    row = lax.broadcasted_iota(jnp.int32, (CH, 128), 0)
    pick = (lane == row + CH * lax.rem(seq_index(), 8)).astype(F32).astype(BF)
    for branch in range(3):
        rows = total[:, branch * 128 : (branch + 1) * 128].astype(BF)
        table[branch * CH : (branch + 1) * CH, :] = mm(pick, rows, (((1,), (1,)), ((), ())))


def vocab(embed_table, in_weight):
    hbm = pl.BlockSpec(memory_space=pltpu.HBM)
    return pl.pallas_call(
        vocab_kernel,
        out_shape=jax.ShapeDtypeStruct((3 * CH, 512), F32),
        in_specs=[hbm, hbm],
        out_specs=pl.BlockSpec(memory_space=pltpu.VMEM),
        scratch_shapes=[
            pltpu.VMEM((512, 4096), BF),
            pltpu.VMEM((4096, 384), BF),
            pltpu.SemaphoreType.DMA((4 * STEPS,)),
        ],
        compiler_params=pltpu.CompilerParams(vmem_limit_bytes=16 << 20),
        cost_estimate=pl.CostEstimate(flops=2 * 512 * 4096 * 384, bytes_accessed=8 << 20, transcendentals=0),
        name="vocab",
    )(in_hbm(embed_table), in_hbm(in_weight.transpose(1, 0, 2)))


def convolve_kernel(
    recv, table, *refs,
):
    sources, (out, taps, token, gated, other, shaped, spec_high, spec_low, lags) = refs[:7], refs[7:16]
    short, direct, first_signal, first_filter, twiddle, second, last = held = refs[16:23]
    copies = [
        pltpu.make_async_copy(source, target, refs[23].at[index])
        for index, (source, target) in enumerate(zip(sources, held))
    ]
    for copy in copies:
        copy.start()
    copies[0].wait()
    copies[1].wait()
    seq, core = seq_index(), lax.axis_index("core")
    lane = lax.broadcasted_iota(jnp.int32, (CH, 256), 1)
    row = lax.broadcasted_iota(jnp.int32, (CH, 256), 0)
    mine = lane == row + CH * seq
    for index in range(10):
        wide = short[index // 3, index % 3 : index % 3 + 1, :] if index < 9 else direct[...]
        column = jnp.sum(jnp.where(mine, wide, 0.0), axis=1, keepdims=True)
        taps[index * CH : (index + 1) * CH, :] = jnp.broadcast_to(column, (CH, 128))

    for source in range(16):
        digits = recv[source, :, 512:].astype(F32)
        token[source * 8 : source * 8 + 8, :] = (digits[:8] * 16.0 + digits[8:]).astype(jnp.int32)
        for q in range(4):
            rows = slice(q * 256 + source * CH, q * 256 + (source + 1) * CH)
            lags[rows, :] = recv[source, :, q * 128 : (q + 1) * 128].astype(F32)

    banks = jnp.concatenate([table[:, i * 128 : (i + 1) * 128] for i in range(4)], 0).astype(BF)
    line = lax.broadcasted_iota(jnp.int32, (256, 256), 0)
    lane = lax.broadcasted_iota(jnp.int32, (256, 256), 1)
    shift = (line == jnp.where(lane < 128, lane + 127, lane - 2)).astype(F32).astype(BF)
    entry = lax.broadcasted_iota(jnp.int32, (128, 128), 0)

    def select(source, before):
        rows = [token[pl.ds(source * 8 + q, 1), :] for q in range(4)]
        chosen = [(entry == jnp.bitwise_and(row, 127)).astype(F32).astype(BF) for row in rows]
        found = mm(banks, jnp.concatenate(chosen, 1))
        bank = jnp.right_shift(jnp.concatenate(rows, 1), 7)
        value = found[: 3 * CH]
        for i in range(1, 4):
            value = jnp.where(bank == i, found[i * 3 * CH : (i + 1) * 3 * CH], value)
        narrow = value.astype(BF)
        blocks = [before] + [narrow[:, q * 128 : (q + 1) * 128] for q in range(4)]
        pairs = [jnp.concatenate([blocks[q], blocks[q + 1]], 1) for q in range(4)]
        lagged = mm(jnp.concatenate(pairs, 0), shift)
        for q in range(4):
            lag = lagged[q * 3 * CH : (q + 1) * 3 * CH]
            filtered = taps[: 3 * CH, :] * value[:, q * 128 : (q + 1) * 128]
            filtered = filtered + taps[3 * CH : 6 * CH, :] * lag[:, :128]
            filtered = filtered + taps[6 * CH : 9 * CH, :] * lag[:, 128:]
            at = pl.ds(pl.multiple_of((source * 4 + q) * CH, CH), CH)
            gated[at, :] = filtered[:CH] * filtered[2 * CH :]
            other[at, :] = filtered[CH : 2 * CH]
        return blocks[4]

    lax.fori_loop(0, 16, select, jnp.zeros((3 * CH, 128), BF), unroll=UNROLL)

    for copy in copies[2:]:
        copy.wait()
    cos_turn, sin_turn = twiddle[0], twiddle[1]
    rows_all = CH * HALF

    def turned(stage, sign):
        real, imag = stage[:HALF], stage[HALF:]
        return jnp.concatenate(
            [real * cos_turn - sign * imag * sin_turn, sign * real * sin_turn + imag * cos_turn], 1
        )

    for pair in range(CH // 2):
        signal = jnp.concatenate(
            [gated[pl.ds(2 * pair + i, 64, stride=CH), :] for i in range(2)], 1
        )
        high, low = halves(signal)
        stage = mm(first_signal[...], jnp.concatenate([high, low, high, high], 0))
        spectrum = jnp.concatenate([turned(stage[:, :128], 1), turned(stage[:, 128:], 1)], 0)
        at = slice(pair * 2 * HALF, (pair + 1) * 2 * HALF)
        spec_high[at, :], spec_low[at, :] = halves(spectrum)

        kernel = jnp.concatenate(
            [lags[pl.ds(2 * pair + i, 64, stride=CH), :] for i in range(2)], 1
        ).astype(BF)
        stage = mm(first_filter[...], jnp.concatenate([kernel, kernel], 0))
        spectrum = jnp.concatenate([turned(stage[:, :128], 1), turned(stage[:, 128:], 1)], 0)
        at = slice(rows_all + pair * 2 * HALF, rows_all + (pair + 1) * 2 * HALF)
        spec_high[at, :], spec_low[at, :] = halves(spectrum)

    def transform(at, dims):
        high, low = spec_high[at, :], spec_low[at, :]
        return mm(high, second[0], dims) + (mm(low, second[0], dims) + mm(high, second[1], dims))

    straight, flipped = (((1,), (0,)), ((), ())), (((1,), (1,)), ((), ()))
    span = 2 * HALF
    for start in range(0, CH // 2, GROUP):
        at = slice(start * span, (start + GROUP) * span)
        left = transform(at, straight)
        right = transform(slice(rows_all + at.start, rows_all + at.stop), straight)
        left_real, left_imag, right_real, right_imag = left[:, :128], left[:, 128:], right[:, :128], right[:, 128:]
        product = jnp.concatenate(
            [left_real * right_real - left_imag * right_imag, left_real * right_imag + left_imag * right_real], 1
        )
        spec_high[at, :], spec_low[at, :] = halves(product)

    for start in range(0, CH // 2, GROUP):
        backs = transform(slice(start * span, (start + GROUP) * span), flipped)
        for pair in range(start, start + GROUP):
            columns = []
            for i in range(2):
                top = ((pair - start) * 2 + i) * HALF
                real, imag = backs[top : top + HALF, :128], backs[top : top + HALF, 128:]
                columns.append(
                    jnp.concatenate([real * cos_turn + imag * sin_turn, imag * cos_turn - real * sin_turn], 0)
                )
            high, low = halves(jnp.concatenate(columns, 1))
            result = mm(last[...], jnp.concatenate([high, low, high, high[:80]], 0))
            for i in range(2):
                shaped[pl.ds(2 * pair + i, 64, stride=CH), :] = result[:, i * 128 : (i + 1) * 128]

    skip = taps[9 * CH :, :]
    low_half = lax.broadcasted_iota(jnp.int32, (CH, 128), 1) < 64
    for a, top, core_to, h in itertools.product(range(2), range(2), range(2), range(4)):
        done = []
        for zl in range(2):
            shard = 8 * a + top * 4 + zl * 2 + core_to
            rows = slice((4 * shard + h) * CH, (4 * shard + h + 1) * CH)
            done.append(other[rows, :] * (shaped[rows, :] + skip * gated[rows, :]))
        first, then = done
        even = jnp.where(low_half, first, pltpu.roll(then, 64, 1)).astype(BF)
        odd = jnp.where(low_half, pltpu.roll(first, 64, 1), then).astype(BF)
        half = jnp.bitwise_xor(core, core_to) if core_to else core
        columns = pl.ds(pl.multiple_of(half * 256 + top * 128, 128), 128)
        for to_y, to_z in itertools.product(range(2), range(2)):
            out[a, to_y, to_z, 2 * h, :, columns] = even
            out[a, to_y, to_z, 2 * h + 1, :, columns] = odd


def convolve(recv, table, short_filter, skip_gain):
    consts = [jnp.asarray(c) for c in tables()]
    whole, hbm = pl.BlockSpec(memory_space=pltpu.VMEM), pl.BlockSpec(memory_space=pltpu.HBM)
    positions = 8192
    fetched = [short_filter, skip_gain[None, :], *consts]
    return pl.pallas_call(
        convolve_kernel,
        out_shape=jax.ShapeDtypeStruct((2, 2, 2, 8, CH, 512), BF),
        in_specs=[whole] * 2 + [hbm] * 7,
        out_specs=whole,
        scratch_shapes=[
            pltpu.VMEM((10 * CH, 128), F32),
            pltpu.VMEM((128, 128), jnp.int32),
            pltpu.VMEM((positions // 128 * CH, 128), F32),
            pltpu.VMEM((positions // 128 * CH, 128), F32),
            pltpu.VMEM((positions // 128 * CH, 128), F32),
            pltpu.VMEM((2 * CH * HALF, 256), BF),
            pltpu.VMEM((2 * CH * HALF, 256), BF),
            pltpu.VMEM((64 * CH, 128), F32),
            *[pltpu.VMEM(array.shape, array.dtype) for array in fetched],
            pltpu.SemaphoreType.DMA((len(fetched),)),
        ],
        cost_estimate=pl.CostEstimate(flops=4 << 30, bytes_accessed=4 << 20, transcendentals=0),
        compiler_params=pltpu.CompilerParams(vmem_limit_bytes=20 << 20),
        name="convolve",
    )(recv, table, *[in_hbm(array) for array in fetched])


def project_kernel(recv, *refs):
    weights, keep, send = refs[:4], refs[4], refs[5]
    chan = lax.axis_index("x") * 2 + lax.axis_index("zh")
    total = None
    for index in range(4):
        lhs = jnp.concatenate(
            [recv[:, jnp.bitwise_xor(chan, 2 * index + i)].reshape(128, 512) for i in range(2)], 0
        )
        part = mm(lhs, weights[index][...], (((0,), (0,)), ((), ())))
        total = part if total is None else total + part
    keep[...] = total[:256]
    send[...] = total[256:].astype(BF)


def project(recv, weights):
    whole = pl.BlockSpec(memory_space=pltpu.VMEM)
    return pl.pallas_call(
        project_kernel,
        out_shape=(jax.ShapeDtypeStruct((256, 1024), F32), jax.ShapeDtypeStruct((256, 1024), BF)),
        in_specs=[whole] * 5,
        out_specs=(whole, whole),
        cost_estimate=pl.CostEstimate(flops=1 << 30, bytes_accessed=5 << 20, transcendentals=0),
        compiler_params=pltpu.CompilerParams(vmem_limit_bytes=20 << 20),
        name="project",
    )(recv.reshape(8, 8, CH, 512), *weights)


def combine_kernel(keep, came, *outs):
    for index, out in enumerate(outs):
        block = jnp.bitwise_xor(column_index(), index)
        rows = pl.ds(pl.multiple_of(block * 64, 64), 64)
        out[...] = (keep[rows, :] + came[rows, :].astype(F32)).astype(BF)


def combine(keep, came):
    whole = pl.BlockSpec(memory_space=pltpu.VMEM)
    return pl.pallas_call(
        combine_kernel,
        out_shape=(jax.ShapeDtypeStruct((64, 1024), BF),) * 4,
        in_specs=[whole, whole],
        out_specs=(whole,) * 4,
        cost_estimate=pl.CostEstimate(flops=1 << 18, bytes_accessed=2 << 20, transcendentals=0),
        compiler_params=pltpu.CompilerParams(vmem_limit_bytes=6 << 20),
        name="combine",
    )(keep, came)


def assemble_kernel(*refs):
    out = refs[-1]
    for index, piece in enumerate(refs[:-1]):
        block = jnp.bitwise_xor(column_index(), index)
        out[:, pl.ds(pl.multiple_of(block * 1024, 1024), 1024)] = piece[...]


def assemble(pieces):
    whole = pl.BlockSpec(memory_space=pltpu.VMEM)
    return pl.pallas_call(
        assemble_kernel,
        out_shape=jax.ShapeDtypeStruct((64, 4096), BF),
        in_specs=[whole] * 4,
        out_specs=whole,
        cost_estimate=pl.CostEstimate(flops=0, bytes_accessed=1 << 20, transcendentals=0),
        compiler_params=pltpu.CompilerParams(vmem_limit_bytes=4 << 20),
        name="assemble",
    )(*pieces)


def permuted(block, move):
    pairs = []
    for place in itertools.product(*[range(SIZES[axis]) for axis in AXES]):
        here = dict(zip(AXES, place))
        there = {**here, **move(here)}
        index = [0, 0]
        for axis in AXES:
            index = [index[0] * SIZES[axis] + here[axis], index[1] * SIZES[axis] + there[axis]]
        pairs.append(tuple(index))
    return lax.ppermute(block, AXES, pairs)


def body(token_ids, embed_table, in_weight, short_filter, long_filter, skip_gain, out_weight):
    payload, held = pack(long_filter, token_ids, out_weight)
    held = held.reshape(128, 1024)
    across = permuted(held, lambda d: {"zh": d["zh"] ^ 1})
    both = jnp.concatenate([held, across], 0)
    weights = [both]
    for index in range(1, 4):
        weights.append(permuted(both, lambda d: {"x": d["x"] ^ index}))
    recv = lax.all_to_all(payload, SEQ, 0, 0, tiled=True)
    table = vocab(embed_table, in_weight)
    chunks = convolve(recv, table, short_filter, skip_gain)
    recv = lax.all_to_all(chunks.reshape(64, CH, 512), ("y", "zl", "x", "zh"), 0, 0, tiled=True)
    keep, send = project(recv, weights)
    came = permuted(send, lambda d: {"core": 1 - d["core"]})
    pieces = list(combine(keep, came))
    for index in range(1, 4):
        pieces[index] = permuted(pieces[index], lambda d: {"y": d["y"] ^ (index // 2), "zl": d["zl"] ^ (index % 2)})
    return assemble(pieces)


def solution(mesh):
    fine = Mesh(mesh.devices.reshape(tuple(SIZES.values())), AXES)
    return jax.shard_map(
        body,
        mesh=fine,
        in_specs=(
            P(SEQ),
            P(),
            P(None, None, CHAN),
            P(None, None, CHAN),
            P(SEQ, CHAN),
            P(CHAN),
            P(CHAN, None),
        ),
        out_specs=P(AXES, None),
        check_vma=False,
    )
```

```python
import functools
import itertools

import jax
import jax.numpy as jnp
import ml_dtypes
import numpy as np
from jax import lax
from jax.experimental import pallas as pl
from jax.experimental.pallas import tpu as pltpu
from jax.sharding import Mesh
from jax.sharding import PartitionSpec as P


SIZES = {"y": 4, "zl": 2, "core": 2, "x": 4, "zh": 2}
AXES = tuple(SIZES)
SEQ, CHAN = ("y", "zl", "core"), ("x", "zh")

N1 = 128
HALF = 72
CH = 16
BF, F32 = jnp.bfloat16, jnp.float32


def split_np(array):
    high = array.astype(np.float32).astype(ml_dtypes.bfloat16)
    low = (array - high.astype(np.float64)).astype(np.float32).astype(ml_dtypes.bfloat16)
    return high, low


@functools.cache
def tables():
    full = 2 * 8192
    freq = np.arange(HALF)[:, None]
    valid = (freq <= N1 // 2).astype(np.float64)
    block = np.arange(64)[None, :]
    angle = 2 * np.pi * (freq * block % N1) / N1
    first = np.concatenate([np.cos(angle) * valid, -np.sin(angle) * valid], 0)
    high, low = split_np(first)
    zero = np.zeros_like(high)
    first_signal = np.concatenate([high, high, low, zero], 1)
    rank = np.arange(64)
    order = 4 * (rank % 16) + rank // 16
    first_filter = np.concatenate([high[:, order], low[:, order]], 1)
    lane = np.arange(128)[None, :]
    turn = 2 * np.pi * (freq * lane) / full
    twiddle = np.stack([np.cos(turn) * valid, -np.sin(turn) * valid]).astype(np.float32)
    pair = 2 * np.pi * (np.arange(128)[:, None] * lane % 128) / 128
    cosine, sine = np.cos(pair), np.sin(pair)
    second = np.concatenate(
        [np.concatenate([cosine, -sine], 1), np.concatenate([sine, cosine], 1)], 0
    )
    second = np.stack(split_np(second))
    weight = np.where((freq == 0) | (freq == N1 // 2), 1.0, 2.0) * valid / full
    last = np.concatenate([np.cos(angle) * weight, -np.sin(angle) * weight], 0).T
    high, low = split_np(last)
    last = np.concatenate([high, high, low, np.zeros((64, 80), high.dtype)], 1)
    return first_signal, first_filter, twiddle, second, last


def halves(value):
    high = value.astype(BF)
    return high, (value - high.astype(F32)).astype(BF)


def mm(left, right, dims=(((1,), (0,)), ((), ()))):
    return lax.dot_general(left, right, dims, preferred_element_type=F32)


def in_hbm(array):
    return pltpu.with_memory_space_constraint(array, pltpu.HBM)


def seq_index():
    return (lax.axis_index("y") * 2 + lax.axis_index("zl")) * 2 + lax.axis_index("core")


def column_index():
    return lax.rem(lax.axis_index("y"), 2) * 2 + lax.axis_index("zl")


def pack_kernel(filt_hbm, tokens_hbm, weight_hbm, payload, held, filt, tokens, sems):
    parts = 4
    mine = weight_hbm.at[
        :,
        pl.ds(pl.multiple_of(lax.axis_index("core") * CH, CH), CH),
        pl.ds(pl.multiple_of(column_index() * 1024, 1024), 1024),
    ]
    rows = 512 // parts
    copies = [
        pltpu.make_async_copy(filt_hbm.at[i * rows : (i + 1) * rows], filt.at[i * rows : (i + 1) * rows], sems.at[i])
        for i in range(parts)
    ]
    copies.append(pltpu.make_async_copy(tokens_hbm, tokens, sems.at[parts]))
    copies.append(pltpu.make_async_copy(mine, held, sems.at[parts + 1]))
    for copy in copies:
        copy.start()
    copies[parts].wait()
    high = jnp.right_shift(tokens[...], 4)
    low = jnp.bitwise_and(tokens[...], 15)
    gap = jnp.zeros((4, 128), F32)
    digits = jnp.concatenate([high.astype(F32), gap, low.astype(F32), gap], 0).astype(BF)
    payload[:, :, 512:] = jnp.broadcast_to(digits[None], (16, CH, 128))
    for i in range(parts):
        copies[i].wait()
        at = slice(i * rows, (i + 1) * rows)
        payload[:, :, at] = filt[at, :].T.astype(BF).reshape(16, CH, rows)
    copies[parts + 1].wait()


def pack(long_filter, token_ids, out_weight):
    hbm, whole = pl.BlockSpec(memory_space=pltpu.HBM), pl.BlockSpec(memory_space=pltpu.VMEM)
    return pl.pallas_call(
        pack_kernel,
        out_shape=(
            jax.ShapeDtypeStruct((16, CH, 640), BF),
            jax.ShapeDtypeStruct((8, CH, 1024), BF),
        ),
        in_specs=[hbm] * 3,
        out_specs=(whole, whole),
        scratch_shapes=[
            pltpu.VMEM((512, 256), F32),
            pltpu.VMEM((4, 128), jnp.int32),
            pltpu.SemaphoreType.DMA((6,)),
        ],
        cost_estimate=pl.CostEstimate(flops=1 << 18, bytes_accessed=1 << 20, transcendentals=0),
        compiler_params=pltpu.CompilerParams(vmem_limit_bytes=6 << 20),
        name="pack",
    )(in_hbm(long_filter), in_hbm(token_ids.reshape(4, 128)), in_hbm(out_weight.reshape(8, 2 * CH, 4096)))


STEPS = 4
GROUP = 8
UNROLL = 16


def vocab_kernel(embed_hbm, weight_hbm, table, embed, weight, sems):
    depth = 4096 // STEPS
    lanes = pl.ds(pl.multiple_of(lax.div(seq_index(), 8) * 128, 128), 128)
    copies = []
    for step in range(STEPS):
        at = slice(step * depth, (step + 1) * depth)
        pair = [pltpu.make_async_copy(embed_hbm.at[:, at], embed.at[:, at], sems.at[4 * step + 3])]
        for branch in range(3):
            pair.append(
                pltpu.make_async_copy(
                    weight_hbm.at[branch, at, lanes],
                    weight.at[at, branch * 128 : (branch + 1) * 128],
                    sems.at[4 * step + branch],
                )
            )
        copies.append(pair)
    for pair in copies:
        for copy in pair:
            copy.start()
    total = None
    for step, pair in enumerate(copies):
        for copy in pair:
            copy.wait()
        at = slice(step * depth, (step + 1) * depth)
        part = mm(embed[:, at], weight[at, :])
        total = part if total is None else total + part
    lane = lax.broadcasted_iota(jnp.int32, (CH, 128), 1)
    row = lax.broadcasted_iota(jnp.int32, (CH, 128), 0)
    pick = (lane == row + CH * lax.rem(seq_index(), 8)).astype(F32).astype(BF)
    for branch in range(3):
        rows = total[:, branch * 128 : (branch + 1) * 128].astype(BF)
        table[branch * CH : (branch + 1) * CH, :] = mm(pick, rows, (((1,), (1,)), ((), ())))


def vocab(embed_table, in_weight):
    hbm = pl.BlockSpec(memory_space=pltpu.HBM)
    return pl.pallas_call(
        vocab_kernel,
        out_shape=jax.ShapeDtypeStruct((3 * CH, 512), F32),
        in_specs=[hbm, hbm],
        out_specs=pl.BlockSpec(memory_space=pltpu.VMEM),
        scratch_shapes=[
            pltpu.VMEM((512, 4096), BF),
            pltpu.VMEM((4096, 384), BF),
            pltpu.SemaphoreType.DMA((4 * STEPS,)),
        ],
        compiler_params=pltpu.CompilerParams(vmem_limit_bytes=16 << 20),
        cost_estimate=pl.CostEstimate(flops=2 * 512 * 4096 * 384, bytes_accessed=8 << 20, transcendentals=0),
        name="vocab",
    )(in_hbm(embed_table), in_hbm(in_weight.transpose(1, 0, 2)))


def convolve_kernel(
    recv, table, *refs,
):
    sources, (out, taps, token, gated, other, shaped, spec_high, spec_low, lags) = refs[:7], refs[7:16]
    short, direct, first_signal, first_filter, twiddle, second, last = held = refs[16:23]
    chunk, out_sems = refs[24:]
    copies = [
        pltpu.make_async_copy(source, target, refs[23].at[index])
        for index, (source, target) in enumerate(zip(sources, held))
    ]
    for copy in copies:
        copy.start()
    copies[0].wait()
    copies[1].wait()
    seq, core = seq_index(), lax.axis_index("core")
    lane = lax.broadcasted_iota(jnp.int32, (CH, 256), 1)
    row = lax.broadcasted_iota(jnp.int32, (CH, 256), 0)
    mine = lane == row + CH * seq
    for index in range(10):
        wide = short[index // 3, index % 3 : index % 3 + 1, :] if index < 9 else direct[...]
        column = jnp.sum(jnp.where(mine, wide, 0.0), axis=1, keepdims=True)
        taps[index * CH : (index + 1) * CH, :] = jnp.broadcast_to(column, (CH, 128))

    for source in range(16):
        digits = recv[source, :, 512:].astype(F32)
        token[source * 8 : source * 8 + 8, :] = (digits[:8] * 16.0 + digits[8:]).astype(jnp.int32)
        for q in range(4):
            rows = slice(q * 256 + source * CH, q * 256 + (source + 1) * CH)
            lags[rows, :] = recv[source, :, q * 128 : (q + 1) * 128].astype(F32)

    banks = jnp.concatenate([table[:, i * 128 : (i + 1) * 128] for i in range(4)], 0).astype(BF)
    line = lax.broadcasted_iota(jnp.int32, (256, 256), 0)
    lane = lax.broadcasted_iota(jnp.int32, (256, 256), 1)
    shift = (line == jnp.where(lane < 128, lane + 127, lane - 2)).astype(F32).astype(BF)
    entry = lax.broadcasted_iota(jnp.int32, (128, 128), 0)

    def select(source, before):
        rows = [token[pl.ds(source * 8 + q, 1), :] for q in range(4)]
        chosen = [(entry == jnp.bitwise_and(row, 127)).astype(F32).astype(BF) for row in rows]
        found = mm(banks, jnp.concatenate(chosen, 1))
        bank = jnp.right_shift(jnp.concatenate(rows, 1), 7)
        value = found[: 3 * CH]
        for i in range(1, 4):
            value = jnp.where(bank == i, found[i * 3 * CH : (i + 1) * 3 * CH], value)
        narrow = value.astype(BF)
        blocks = [before] + [narrow[:, q * 128 : (q + 1) * 128] for q in range(4)]
        pairs = [jnp.concatenate([blocks[q], blocks[q + 1]], 1) for q in range(4)]
        lagged = mm(jnp.concatenate(pairs, 0), shift)
        for q in range(4):
            lag = lagged[q * 3 * CH : (q + 1) * 3 * CH]
            filtered = taps[: 3 * CH, :] * value[:, q * 128 : (q + 1) * 128]
            filtered = filtered + taps[3 * CH : 6 * CH, :] * lag[:, :128]
            filtered = filtered + taps[6 * CH : 9 * CH, :] * lag[:, 128:]
            at = pl.ds(pl.multiple_of((source * 4 + q) * CH, CH), CH)
            gated[at, :] = filtered[:CH] * filtered[2 * CH :]
            other[at, :] = filtered[CH : 2 * CH]
        return blocks[4]

    lax.fori_loop(0, 16, select, jnp.zeros((3 * CH, 128), BF), unroll=UNROLL)

    for copy in copies[2:]:
        copy.wait()
    cos_turn, sin_turn = twiddle[0], twiddle[1]
    rows_all = CH * HALF

    def turned(stage, sign):
        real, imag = stage[:HALF], stage[HALF:]
        return jnp.concatenate(
            [real * cos_turn - sign * imag * sin_turn, sign * real * sin_turn + imag * cos_turn], 1
        )

    for pair in range(CH // 2):
        signal = jnp.concatenate(
            [gated[pl.ds(2 * pair + i, 64, stride=CH), :] for i in range(2)], 1
        )
        high, low = halves(signal)
        stage = mm(first_signal[...], jnp.concatenate([high, low, high, high], 0))
        spectrum = jnp.concatenate([turned(stage[:, :128], 1), turned(stage[:, 128:], 1)], 0)
        at = slice(pair * 2 * HALF, (pair + 1) * 2 * HALF)
        spec_high[at, :], spec_low[at, :] = halves(spectrum)

        kernel = jnp.concatenate(
            [lags[pl.ds(2 * pair + i, 64, stride=CH), :] for i in range(2)], 1
        ).astype(BF)
        stage = mm(first_filter[...], jnp.concatenate([kernel, kernel], 0))
        spectrum = jnp.concatenate([turned(stage[:, :128], 1), turned(stage[:, 128:], 1)], 0)
        at = slice(rows_all + pair * 2 * HALF, rows_all + (pair + 1) * 2 * HALF)
        spec_high[at, :], spec_low[at, :] = halves(spectrum)

    def transform(at, dims):
        high, low = spec_high[at, :], spec_low[at, :]
        return mm(high, second[0], dims) + (mm(low, second[0], dims) + mm(high, second[1], dims))

    straight, flipped = (((1,), (0,)), ((), ())), (((1,), (1,)), ((), ()))
    span = 2 * HALF
    for start in range(0, CH // 2, GROUP):
        at = slice(start * span, (start + GROUP) * span)
        left = transform(at, straight)
        right = transform(slice(rows_all + at.start, rows_all + at.stop), straight)
        left_real, left_imag, right_real, right_imag = left[:, :128], left[:, 128:], right[:, :128], right[:, 128:]
        product = jnp.concatenate(
            [left_real * right_real - left_imag * right_imag, left_real * right_imag + left_imag * right_real], 1
        )
        spec_high[at, :], spec_low[at, :] = halves(product)

    for start in range(0, CH // 2, GROUP):
        backs = transform(slice(start * span, (start + GROUP) * span), flipped)
        for pair in range(start, start + GROUP):
            columns = []
            for i in range(2):
                top = ((pair - start) * 2 + i) * HALF
                real, imag = backs[top : top + HALF, :128], backs[top : top + HALF, 128:]
                columns.append(
                    jnp.concatenate([real * cos_turn + imag * sin_turn, imag * cos_turn - real * sin_turn], 0)
                )
            high, low = halves(jnp.concatenate(columns, 1))
            result = mm(last[...], jnp.concatenate([high, low, high, high[:80]], 0))
            for i in range(2):
                shaped[pl.ds(2 * pair + i, 64, stride=CH), :] = result[:, i * 128 : (i + 1) * 128]

    skip = taps[9 * CH :, :]
    low_half = lax.broadcasted_iota(jnp.int32, (CH, 128), 1) < 64
    copies = []
    for a, h in itertools.product(range(2), range(4)):
        for top, core_to in itertools.product(range(2), range(2)):
            done = []
            for zl in range(2):
                shard = 8 * a + top * 4 + zl * 2 + core_to
                rows = slice((4 * shard + h) * CH, (4 * shard + h + 1) * CH)
                done.append(other[rows, :] * (shaped[rows, :] + skip * gated[rows, :]))
            first, then = done
            half = jnp.bitwise_xor(core, core_to) if core_to else core
            columns = pl.ds(pl.multiple_of(half * 256 + top * 128, 128), 128)
            chunk[a * 8 + 2 * h, :, columns] = jnp.where(low_half, first, pltpu.roll(then, 64, 1)).astype(BF)
            chunk[a * 8 + 2 * h + 1, :, columns] = jnp.where(low_half, pltpu.roll(first, 64, 1), then).astype(BF)
        for member in range(4):
            copies.append(
                pltpu.make_async_copy(
                    chunk.at[a * 8 + 2 * h : a * 8 + 2 * h + 2],
                    out.at[pl.ds((a * 4 + member) * 8 + 2 * h, 2)],
                    out_sems.at[(a * 4 + h) * 4 + member],
                )
            )
            copies[-1].start()
    for copy in copies:
        copy.wait()


def convolve(recv, table, short_filter, skip_gain):
    consts = [jnp.asarray(c) for c in tables()]
    whole, hbm = pl.BlockSpec(memory_space=pltpu.VMEM), pl.BlockSpec(memory_space=pltpu.HBM)
    positions = 8192
    fetched = [short_filter, skip_gain[None, :], *consts]
    return pl.pallas_call(
        convolve_kernel,
        out_shape=pltpu.HBM((64, CH, 512), BF),
        in_specs=[whole] * 2 + [hbm] * 7,
        out_specs=hbm,
        scratch_shapes=[
            pltpu.VMEM((10 * CH, 128), F32),
            pltpu.VMEM((128, 128), jnp.int32),
            pltpu.VMEM((positions // 128 * CH, 128), F32),
            pltpu.VMEM((positions // 128 * CH, 128), F32),
            pltpu.VMEM((positions // 128 * CH, 128), F32),
            pltpu.VMEM((2 * CH * HALF, 256), BF),
            pltpu.VMEM((2 * CH * HALF, 256), BF),
            pltpu.VMEM((64 * CH, 128), F32),
            *[pltpu.VMEM(array.shape, array.dtype) for array in fetched],
            pltpu.SemaphoreType.DMA((len(fetched),)),
            pltpu.VMEM((16, CH, 512), BF),
            pltpu.SemaphoreType.DMA((32,)),
        ],
        cost_estimate=pl.CostEstimate(flops=4 << 30, bytes_accessed=4 << 20, transcendentals=0),
        compiler_params=pltpu.CompilerParams(vmem_limit_bytes=20 << 20),
        name="convolve",
    )(recv, table, *[in_hbm(array) for array in fetched])


def project_kernel(half, recv, own, one, upper, lower, three, out):
    chan = lax.axis_index("x") * 2 + lax.axis_index("zh")
    total = None
    for index in range(4):
        lhs = jnp.concatenate(
            [
                recv[:, jnp.bitwise_xor(chan, 2 * index + i), :, half * 256 : (half + 1) * 256].reshape(128, 256)
                for i in range(2)
            ],
            0,
        )
        rhs = jnp.concatenate([upper[...], lower[...]], 0) if index == 2 else (own, one, None, three)[index][...]
        part = mm(lhs, rhs, (((0,), (0,)), ((), ())))
        total = part if total is None else total + part
    out[...] = total.astype(out.dtype)


def project(recv, weights, half):
    whole = pl.BlockSpec(memory_space=pltpu.VMEM)
    return pl.pallas_call(
        functools.partial(project_kernel, half),
        out_shape=jax.ShapeDtypeStruct((256, 1024), BF if half else F32),
        in_specs=[whole] * 6,
        out_specs=whole,
        cost_estimate=pl.CostEstimate(flops=1 << 29, bytes_accessed=4 << 20, transcendentals=0),
        compiler_params=pltpu.CompilerParams(vmem_limit_bytes=20 << 20),
        name="send" if half else "keep",
    )(recv.reshape(8, 8, CH, 512), *weights)


def combine_kernel(keep, came, *outs):
    for index, out in enumerate(outs):
        block = jnp.bitwise_xor(column_index(), index)
        rows = pl.ds(pl.multiple_of(block * 64, 64), 64)
        out[...] = (keep[rows, :] + came[rows, :].astype(F32)).astype(BF)


def combine(keep, came):
    whole = pl.BlockSpec(memory_space=pltpu.VMEM)
    return pl.pallas_call(
        combine_kernel,
        out_shape=(jax.ShapeDtypeStruct((64, 1024), BF),) * 4,
        in_specs=[whole, whole],
        out_specs=(whole,) * 4,
        cost_estimate=pl.CostEstimate(flops=1 << 18, bytes_accessed=2 << 20, transcendentals=0),
        compiler_params=pltpu.CompilerParams(vmem_limit_bytes=6 << 20),
        name="combine",
    )(keep, came)


def assemble_kernel(*refs):
    out = refs[-1]
    for index, piece in enumerate(refs[:-1]):
        block = jnp.bitwise_xor(column_index(), index)
        out[:, pl.ds(pl.multiple_of(block * 1024, 1024), 1024)] = piece[...]


def assemble(pieces):
    whole = pl.BlockSpec(memory_space=pltpu.VMEM)
    return pl.pallas_call(
        assemble_kernel,
        out_shape=jax.ShapeDtypeStruct((64, 4096), BF),
        in_specs=[whole] * 4,
        out_specs=whole,
        cost_estimate=pl.CostEstimate(flops=0, bytes_accessed=1 << 20, transcendentals=0),
        compiler_params=pltpu.CompilerParams(vmem_limit_bytes=4 << 20),
        name="assemble",
    )(*pieces)


def permuted(block, move):
    pairs = []
    for place in itertools.product(*[range(SIZES[axis]) for axis in AXES]):
        here = dict(zip(AXES, place))
        there = {**here, **move(here)}
        index = [0, 0]
        for axis in AXES:
            index = [index[0] * SIZES[axis] + here[axis], index[1] * SIZES[axis] + there[axis]]
        pairs.append(tuple(index))
    return lax.ppermute(block, AXES, pairs)


def body(token_ids, embed_table, in_weight, short_filter, long_filter, skip_gain, out_weight):
    payload, held = pack(long_filter, token_ids, out_weight)
    held = held.reshape(128, 1024)
    across = permuted(held, lambda d: {"zh": d["zh"] ^ 1})
    both = jnp.concatenate([held, across], 0)
    beside = {}
    for index in (1, 3):
        beside[index] = permuted(both, lambda d: {"x": d["x"] ^ index})
    recv = lax.all_to_all(payload, SEQ, 0, 0, tiled=True)
    table = vocab(embed_table, in_weight)
    chunks = convolve(recv, table, short_filter, skip_gain)
    recv = lax.all_to_all(chunks, ("y", "zl", "x", "zh"), 0, 0, tiled=True)
    upper = permuted(beside[3][:128], lambda d: {"x": d["x"] ^ 1})
    lower = permuted(beside[1][128:], lambda d: {"x": d["x"] ^ 3})
    weights = [both, beside[1], upper, lower, beside[3]]
    send = project(recv, weights, 1)
    came = permuted(send, lambda d: {"core": 1 - d["core"]})
    keep = project(recv, weights, 0)
    pieces = list(combine(keep, came))
    for index in range(1, 4):
        pieces[index] = permuted(pieces[index], lambda d: {"y": d["y"] ^ (index // 2), "zl": d["zl"] ^ (index % 2)})
    return assemble(pieces)


def solution(mesh):
    fine = Mesh(mesh.devices.reshape(tuple(SIZES.values())), AXES)
    return jax.shard_map(
        body,
        mesh=fine,
        in_specs=(
            P(SEQ),
            P(),
            P(None, None, CHAN),
            P(None, None, CHAN),
            P(SEQ, CHAN),
            P(CHAN),
            P(CHAN, None),
        ),
        out_specs=P(AXES, None),
        check_vma=False,
    )
```

```python
import functools
import itertools

import jax
import jax.numpy as jnp
import ml_dtypes
import numpy as np
from jax import lax
from jax.experimental import pallas as pl
from jax.experimental.pallas import tpu as pltpu
from jax.sharding import Mesh
from jax.sharding import PartitionSpec as P


SIZES = {"y": 4, "zl": 2, "core": 2, "x": 4, "zh": 2}
AXES = tuple(SIZES)
SEQ, CHAN = ("y", "zl", "core"), ("x", "zh")

N1 = 128
HALF = 72
CH = 16
BF, F32 = jnp.bfloat16, jnp.float32


def split_np(array):
    high = array.astype(np.float32).astype(ml_dtypes.bfloat16)
    low = (array - high.astype(np.float64)).astype(np.float32).astype(ml_dtypes.bfloat16)
    return high, low


@functools.cache
def tables():
    full = 2 * 8192
    freq = np.arange(HALF)[:, None]
    valid = (freq <= N1 // 2).astype(np.float64)
    block = np.arange(64)[None, :]
    angle = 2 * np.pi * (freq * block % N1) / N1
    first = np.concatenate([np.cos(angle) * valid, -np.sin(angle) * valid], 0)
    high, low = split_np(first)
    zero = np.zeros_like(high)
    first_signal = np.concatenate([high, high, low, zero], 1)
    rank = np.arange(64)
    order = 4 * (rank % 16) + rank // 16
    first_filter = np.concatenate([high[:, order], low[:, order]], 1)
    lane = np.arange(128)[None, :]
    turn = 2 * np.pi * (freq * lane) / full
    twiddle = np.stack([np.cos(turn) * valid, -np.sin(turn) * valid]).astype(np.float32)
    pair = 2 * np.pi * (np.arange(128)[:, None] * lane % 128) / 128
    cosine, sine = np.cos(pair), np.sin(pair)
    second = np.concatenate(
        [np.concatenate([cosine, -sine], 1), np.concatenate([sine, cosine], 1)], 0
    )
    second = np.stack(split_np(second))
    weight = np.where((freq == 0) | (freq == N1 // 2), 1.0, 2.0) * valid / full
    last = np.concatenate([np.cos(angle) * weight, -np.sin(angle) * weight], 0).T
    high, low = split_np(last)
    last = np.concatenate([high, high, low, np.zeros((64, 80), high.dtype)], 1)
    return first_signal, first_filter, twiddle, second, last


def halves(value):
    high = value.astype(BF)
    return high, (value - high.astype(F32)).astype(BF)


def mm(left, right, dims=(((1,), (0,)), ((), ()))):
    return lax.dot_general(left, right, dims, preferred_element_type=F32)


def in_hbm(array):
    return pltpu.with_memory_space_constraint(array, pltpu.HBM)


def seq_index():
    return (lax.axis_index("y") * 2 + lax.axis_index("zl")) * 2 + lax.axis_index("core")


def column_index():
    return lax.rem(lax.axis_index("y"), 2) * 2 + lax.axis_index("zl")


def pack_kernel(filt_hbm, tokens_hbm, weight_hbm, payload, held, filt, tokens, sems):
    parts = 2
    mine = weight_hbm.at[
        :,
        pl.ds(pl.multiple_of(lax.axis_index("core") * CH, CH), CH),
        pl.ds(pl.multiple_of(column_index() * 1024, 1024), 1024),
    ]
    rows = 512 // parts
    copies = [
        pltpu.make_async_copy(filt_hbm.at[i * rows : (i + 1) * rows], filt.at[i * rows : (i + 1) * rows], sems.at[i])
        for i in range(parts)
    ]
    copies.append(pltpu.make_async_copy(tokens_hbm, tokens, sems.at[parts]))
    copies.append(pltpu.make_async_copy(mine, held, sems.at[parts + 1]))
    for copy in copies:
        copy.start()
    copies[parts].wait()
    high = jnp.right_shift(tokens[...], 4)
    low = jnp.bitwise_and(tokens[...], 15)
    gap = jnp.zeros((4, 128), F32)
    digits = jnp.concatenate([high.astype(F32), gap, low.astype(F32), gap], 0).astype(BF)
    payload[:, :, 512:] = jnp.broadcast_to(digits[None], (16, CH, 128))
    for i in range(parts):
        copies[i].wait()
        at = slice(i * rows, (i + 1) * rows)
        payload[:, :, at] = filt[at, :].T.astype(BF).reshape(16, CH, rows)
    copies[parts + 1].wait()


def pack(long_filter, token_ids, out_weight):
    hbm, whole = pl.BlockSpec(memory_space=pltpu.HBM), pl.BlockSpec(memory_space=pltpu.VMEM)
    return pl.pallas_call(
        pack_kernel,
        out_shape=(
            jax.ShapeDtypeStruct((16, CH, 640), BF),
            jax.ShapeDtypeStruct((8, CH, 1024), BF),
        ),
        in_specs=[hbm] * 3,
        out_specs=(whole, whole),
        scratch_shapes=[
            pltpu.VMEM((512, 256), F32),
            pltpu.VMEM((4, 128), jnp.int32),
            pltpu.SemaphoreType.DMA((4,)),
        ],
        cost_estimate=pl.CostEstimate(flops=1 << 18, bytes_accessed=1 << 20, transcendentals=0),
        compiler_params=pltpu.CompilerParams(vmem_limit_bytes=6 << 20),
        name="pack",
    )(in_hbm(long_filter), in_hbm(token_ids.reshape(4, 128)), in_hbm(out_weight.reshape(8, 2 * CH, 4096)))


STEPS = 4
GROUP = 8
BATCH = 4
UNROLL = 4


def vocab_kernel(embed_hbm, weight_hbm, table, embed, weight, sems):
    depth = 4096 // STEPS
    lanes = pl.ds(pl.multiple_of(lax.div(seq_index(), 8) * 128, 128), 128)
    copies = []
    for step in range(STEPS):
        at = slice(step * depth, (step + 1) * depth)
        pair = [pltpu.make_async_copy(embed_hbm.at[:, at], embed.at[:, at], sems.at[4 * step + 3])]
        for branch in range(3):
            pair.append(
                pltpu.make_async_copy(
                    weight_hbm.at[branch, at, lanes],
                    weight.at[at, branch * 128 : (branch + 1) * 128],
                    sems.at[4 * step + branch],
                )
            )
        copies.append(pair)
    for pair in copies:
        for copy in pair:
            copy.start()
    total = None
    for step, pair in enumerate(copies):
        for copy in pair:
            copy.wait()
        at = slice(step * depth, (step + 1) * depth)
        part = mm(embed[:, at], weight[at, :])
        total = part if total is None else total + part
    lane = lax.broadcasted_iota(jnp.int32, (CH, 128), 1)
    row = lax.broadcasted_iota(jnp.int32, (CH, 128), 0)
    pick = (lane == row + CH * lax.rem(seq_index(), 8)).astype(F32).astype(BF)
    for branch in range(3):
        rows = total[:, branch * 128 : (branch + 1) * 128].astype(BF)
        table[branch * CH : (branch + 1) * CH, :] = mm(pick, rows, (((1,), (1,)), ((), ())))


def vocab(embed_table, in_weight):
    hbm = pl.BlockSpec(memory_space=pltpu.HBM)
    return pl.pallas_call(
        vocab_kernel,
        out_shape=jax.ShapeDtypeStruct((3 * CH, 512), F32),
        in_specs=[hbm, hbm],
        out_specs=pl.BlockSpec(memory_space=pltpu.VMEM),
        scratch_shapes=[
            pltpu.VMEM((512, 4096), BF),
            pltpu.VMEM((4096, 384), BF),
            pltpu.SemaphoreType.DMA((4 * STEPS,)),
        ],
        compiler_params=pltpu.CompilerParams(vmem_limit_bytes=16 << 20),
        cost_estimate=pl.CostEstimate(flops=2 * 512 * 4096 * 384, bytes_accessed=8 << 20, transcendentals=0),
        name="vocab",
    )(in_hbm(embed_table), in_hbm(in_weight.transpose(1, 0, 2)))


def convolve_kernel(
    recv, table, *refs,
):
    sources, (out, taps, token, gated, other, shaped, spec_high, spec_low, lags) = refs[:7], refs[7:16]
    short, direct, first_signal, first_filter, twiddle, second, last = held = refs[16:23]
    chunk, out_sems = refs[24:]
    copies = [
        pltpu.make_async_copy(source, target, refs[23].at[index])
        for index, (source, target) in enumerate(zip(sources, held))
    ]
    for copy in copies:
        copy.start()
    for source in range(16):
        digits = recv[source, :, 512:].astype(F32)
        token[source * 8 : source * 8 + 8, :] = (digits[:8] * 16.0 + digits[8:]).astype(jnp.int32)
        for q in range(4):
            rows = slice(q * 256 + source * CH, q * 256 + (source + 1) * CH)
            lags[rows, :] = recv[source, :, q * 128 : (q + 1) * 128].astype(F32)

    banks = jnp.concatenate([table[:, i * 128 : (i + 1) * 128] for i in range(4)], 0).astype(BF)
    line = lax.broadcasted_iota(jnp.int32, (256, 256), 0)
    lane = lax.broadcasted_iota(jnp.int32, (256, 256), 1)
    shift = (line == jnp.where(lane < 128, lane + 127, lane - 2)).astype(F32).astype(BF)
    entry = lax.broadcasted_iota(jnp.int32, (128, 128), 0)

    copies[0].wait()
    copies[1].wait()
    seq, core = seq_index(), lax.axis_index("core")
    lane = lax.broadcasted_iota(jnp.int32, (CH, 256), 1)
    row = lax.broadcasted_iota(jnp.int32, (CH, 256), 0)
    mine = lane == row + CH * seq
    for index in range(10):
        wide = short[index // 3, index % 3 : index % 3 + 1, :] if index < 9 else direct[...]
        column = jnp.sum(jnp.where(mine, wide, 0.0), axis=1, keepdims=True)
        taps[index * CH : (index + 1) * CH, :] = jnp.broadcast_to(column, (CH, 128))

    def select(step, before):
        blocks = [before]
        for source in range(BATCH):
            rows = [token[pl.ds((step * BATCH + source) * 8 + q, 1), :] for q in range(4)]
            chosen = [(entry == jnp.bitwise_and(row, 127)).astype(F32).astype(BF) for row in rows]
            found = mm(banks, jnp.concatenate(chosen, 1))
            bank = jnp.right_shift(jnp.concatenate(rows, 1), 7)
            value = found[: 3 * CH]
            for i in range(1, 4):
                value = jnp.where(bank == i, found[i * 3 * CH : (i + 1) * 3 * CH], value)
            narrow = value.astype(BF)
            blocks += [narrow[:, q * 128 : (q + 1) * 128] for q in range(4)]
        pairs = [jnp.concatenate([blocks[q], blocks[q + 1]], 1) for q in range(4 * BATCH)]
        lagged = mm(jnp.concatenate(pairs, 0), shift)
        for q in range(4 * BATCH):
            lag = lagged[q * 3 * CH : (q + 1) * 3 * CH]
            filtered = taps[: 3 * CH, :] * blocks[q + 1].astype(F32)
            filtered = filtered + taps[3 * CH : 6 * CH, :] * lag[:, :128]
            filtered = filtered + taps[6 * CH : 9 * CH, :] * lag[:, 128:]
            at = pl.ds(pl.multiple_of((step * 4 * BATCH + q) * CH, CH), CH)
            gated[at, :] = filtered[:CH] * filtered[2 * CH :]
            other[at, :] = filtered[CH : 2 * CH]
        return blocks[-1]

    lax.fori_loop(0, 16 // BATCH, select, jnp.zeros((3 * CH, 128), BF), unroll=UNROLL)

    for copy in copies[2:]:
        copy.wait()
    cos_turn, sin_turn = twiddle[0], twiddle[1]
    rows_all = CH * HALF

    def turned(stage, sign):
        real, imag = stage[:HALF], stage[HALF:]
        return jnp.concatenate(
            [real * cos_turn - sign * imag * sin_turn, sign * real * sin_turn + imag * cos_turn], 1
        )

    for pair in range(CH // 2):
        signal = jnp.concatenate(
            [gated[pl.ds(2 * pair + i, 64, stride=CH), :] for i in range(2)], 1
        )
        high, low = halves(signal)
        stage = mm(first_signal[...], jnp.concatenate([high, low, high, high], 0))
        spectrum = jnp.concatenate([turned(stage[:, :128], 1), turned(stage[:, 128:], 1)], 0)
        at = slice(pair * 2 * HALF, (pair + 1) * 2 * HALF)
        spec_high[at, :], spec_low[at, :] = halves(spectrum)

        kernel = jnp.concatenate(
            [lags[pl.ds(2 * pair + i, 64, stride=CH), :] for i in range(2)], 1
        ).astype(BF)
        stage = mm(first_filter[...], jnp.concatenate([kernel, kernel], 0))
        spectrum = jnp.concatenate([turned(stage[:, :128], 1), turned(stage[:, 128:], 1)], 0)
        at = slice(rows_all + pair * 2 * HALF, rows_all + (pair + 1) * 2 * HALF)
        spec_high[at, :], spec_low[at, :] = halves(spectrum)

    def transform(at, dims):
        high, low = spec_high[at, :], spec_low[at, :]
        return mm(high, second[0], dims) + (mm(low, second[0], dims) + mm(high, second[1], dims))

    straight, flipped = (((1,), (0,)), ((), ())), (((1,), (1,)), ((), ()))
    span = 2 * HALF
    for start in range(0, CH // 2, GROUP):
        at = slice(start * span, (start + GROUP) * span)
        left = transform(at, straight)
        right = transform(slice(rows_all + at.start, rows_all + at.stop), straight)
        left_real, left_imag, right_real, right_imag = left[:, :128], left[:, 128:], right[:, :128], right[:, 128:]
        product = jnp.concatenate(
            [left_real * right_real - left_imag * right_imag, left_real * right_imag + left_imag * right_real], 1
        )
        spec_high[at, :], spec_low[at, :] = halves(product)

    for start in range(0, CH // 2, GROUP):
        backs = transform(slice(start * span, (start + GROUP) * span), flipped)
        for pair in range(start, start + GROUP):
            columns = []
            for i in range(2):
                top = ((pair - start) * 2 + i) * HALF
                real, imag = backs[top : top + HALF, :128], backs[top : top + HALF, 128:]
                columns.append(
                    jnp.concatenate([real * cos_turn + imag * sin_turn, imag * cos_turn - real * sin_turn], 0)
                )
            high, low = halves(jnp.concatenate(columns, 1))
            result = mm(last[...], jnp.concatenate([high, low, high, high[:80]], 0))
            for i in range(2):
                shaped[pl.ds(2 * pair + i, 64, stride=CH), :] = result[:, i * 128 : (i + 1) * 128]

    skip = taps[9 * CH :, :]
    low_half = lax.broadcasted_iota(jnp.int32, (CH, 128), 1) < 64
    copies = []
    for a, h in itertools.product(range(2), range(4)):
        for top, core_to in itertools.product(range(2), range(2)):
            done = []
            for zl in range(2):
                shard = 8 * a + top * 4 + zl * 2 + core_to
                rows = slice((4 * shard + h) * CH, (4 * shard + h + 1) * CH)
                done.append(other[rows, :] * (shaped[rows, :] + skip * gated[rows, :]))
            first, then = done
            half = jnp.bitwise_xor(core, core_to) if core_to else core
            columns = pl.ds(pl.multiple_of(half * 256 + top * 128, 128), 128)
            chunk[a * 8 + 2 * h, :, columns] = jnp.where(low_half, first, pltpu.roll(then, 64, 1)).astype(BF)
            chunk[a * 8 + 2 * h + 1, :, columns] = jnp.where(low_half, pltpu.roll(first, 64, 1), then).astype(BF)
        for member in range(4):
            copies.append(
                pltpu.make_async_copy(
                    chunk.at[a * 8 + 2 * h : a * 8 + 2 * h + 2],
                    out.at[pl.ds((a * 4 + member) * 8 + 2 * h, 2)],
                    out_sems.at[(a * 4 + h) * 4 + member],
                )
            )
            copies[-1].start()
    for copy in copies:
        copy.wait()


def convolve(recv, table, short_filter, skip_gain):
    consts = [jnp.asarray(c) for c in tables()]
    whole, hbm = pl.BlockSpec(memory_space=pltpu.VMEM), pl.BlockSpec(memory_space=pltpu.HBM)
    positions = 8192
    fetched = [short_filter, skip_gain[None, :], *consts]
    return pl.pallas_call(
        convolve_kernel,
        out_shape=pltpu.HBM((64, CH, 512), BF),
        in_specs=[whole] * 2 + [hbm] * 7,
        out_specs=hbm,
        scratch_shapes=[
            pltpu.VMEM((10 * CH, 128), F32),
            pltpu.VMEM((128, 128), jnp.int32),
            pltpu.VMEM((positions // 128 * CH, 128), F32),
            pltpu.VMEM((positions // 128 * CH, 128), F32),
            pltpu.VMEM((positions // 128 * CH, 128), F32),
            pltpu.VMEM((2 * CH * HALF, 256), BF),
            pltpu.VMEM((2 * CH * HALF, 256), BF),
            pltpu.VMEM((64 * CH, 128), F32),
            *[pltpu.VMEM(array.shape, array.dtype) for array in fetched],
            pltpu.SemaphoreType.DMA((len(fetched),)),
            pltpu.VMEM((16, CH, 512), BF),
            pltpu.SemaphoreType.DMA((32,)),
        ],
        cost_estimate=pl.CostEstimate(flops=4 << 30, bytes_accessed=4 << 20, transcendentals=0),
        compiler_params=pltpu.CompilerParams(vmem_limit_bytes=20 << 20),
        name="convolve",
    )(recv, table, *[in_hbm(array) for array in fetched])


def project_kernel(half, recv, own, one, upper, lower, three, out):
    chan = lax.axis_index("x") * 2 + lax.axis_index("zh")
    total = None
    for index in range(4):
        lhs = jnp.concatenate(
            [
                recv[:, jnp.bitwise_xor(chan, 2 * index + i), :, half * 256 : (half + 1) * 256].reshape(128, 256)
                for i in range(2)
            ],
            0,
        )
        rhs = jnp.concatenate([upper[...], lower[...]], 0) if index == 2 else (own, one, None, three)[index][...]
        part = mm(lhs, rhs, (((0,), (0,)), ((), ())))
        total = part if total is None else total + part
    out[...] = total.astype(out.dtype)


def project(recv, weights, half):
    whole = pl.BlockSpec(memory_space=pltpu.VMEM)
    return pl.pallas_call(
        functools.partial(project_kernel, half),
        out_shape=jax.ShapeDtypeStruct((256, 1024), BF if half else F32),
        in_specs=[whole] * 6,
        out_specs=whole,
        cost_estimate=pl.CostEstimate(flops=1 << 29, bytes_accessed=4 << 20, transcendentals=0),
        compiler_params=pltpu.CompilerParams(vmem_limit_bytes=20 << 20),
        name="send" if half else "keep",
    )(recv.reshape(8, 8, CH, 512), *weights)


def combine_kernel(keep, came, *outs):
    for index, out in enumerate(outs):
        block = jnp.bitwise_xor(column_index(), index)
        rows = pl.ds(pl.multiple_of(block * 64, 64), 64)
        out[...] = (keep[rows, :] + came[rows, :].astype(F32)).astype(BF)


def combine(keep, came):
    whole = pl.BlockSpec(memory_space=pltpu.VMEM)
    return pl.pallas_call(
        combine_kernel,
        out_shape=(jax.ShapeDtypeStruct((64, 1024), BF),) * 4,
        in_specs=[whole, whole],
        out_specs=(whole,) * 4,
        cost_estimate=pl.CostEstimate(flops=1 << 18, bytes_accessed=2 << 20, transcendentals=0),
        compiler_params=pltpu.CompilerParams(vmem_limit_bytes=6 << 20),
        name="combine",
    )(keep, came)


def assemble_kernel(*refs):
    pieces, out, sems = refs[:4], refs[4], refs[5]
    copies = []
    for index, piece in enumerate(pieces):
        block = jnp.bitwise_xor(column_index(), index)
        columns = pl.ds(pl.multiple_of(block * 1024, 1024), 1024)
        copies.append(pltpu.make_async_copy(piece, out.at[:, columns], sems.at[index]))
        copies[-1].start()
    for copy in copies:
        copy.wait()


def assemble(pieces):
    anywhere = pl.BlockSpec(memory_space=pl.ANY)
    return pl.pallas_call(
        assemble_kernel,
        out_shape=jax.ShapeDtypeStruct((64, 4096), BF),
        in_specs=[anywhere] * 4,
        out_specs=anywhere,
        scratch_shapes=[pltpu.SemaphoreType.DMA((4,))],
        cost_estimate=pl.CostEstimate(flops=0, bytes_accessed=1 << 20, transcendentals=0),
        compiler_params=pltpu.CompilerParams(vmem_limit_bytes=4 << 20),
        name="assemble",
    )(*pieces)


def permuted(block, move):
    pairs = []
    for place in itertools.product(*[range(SIZES[axis]) for axis in AXES]):
        here = dict(zip(AXES, place))
        there = {**here, **move(here)}
        index = [0, 0]
        for axis in AXES:
            index = [index[0] * SIZES[axis] + here[axis], index[1] * SIZES[axis] + there[axis]]
        pairs.append(tuple(index))
    return lax.ppermute(block, AXES, pairs)


def body(token_ids, embed_table, in_weight, short_filter, long_filter, skip_gain, out_weight):
    payload, held = pack(long_filter, token_ids, out_weight)
    held = held.reshape(128, 1024)
    across = permuted(held, lambda d: {"zh": d["zh"] ^ 1})
    both = jnp.concatenate([held, across], 0)
    beside = {}
    for index in (1, 3):
        beside[index] = permuted(both, lambda d: {"x": d["x"] ^ index})
    recv = lax.all_to_all(payload, SEQ, 0, 0, tiled=True)
    table = vocab(embed_table, in_weight)
    chunks = convolve(recv, table, short_filter, skip_gain)
    recv = lax.all_to_all(chunks, ("y", "zl", "x", "zh"), 0, 0, tiled=True)
    upper = permuted(beside[3][:128], lambda d: {"x": d["x"] ^ 1})
    lower = permuted(beside[1][128:], lambda d: {"x": d["x"] ^ 3})
    weights = [both, beside[1], upper, lower, beside[3]]
    send = project(recv, weights, 1)
    came = permuted(send, lambda d: {"core": 1 - d["core"]})
    keep = project(recv, weights, 0)
    pieces = list(combine(keep, came))
    for index in range(1, 4):
        pieces[index] = permuted(pieces[index], lambda d: {"y": d["y"] ^ (index // 2), "zl": d["zl"] ^ (index % 2)})
    return assemble(pieces)


def solution(mesh):
    fine = Mesh(mesh.devices.reshape(tuple(SIZES.values())), AXES)
    return jax.shard_map(
        body,
        mesh=fine,
        in_specs=(
            P(SEQ),
            P(),
            P(None, None, CHAN),
            P(None, None, CHAN),
            P(SEQ, CHAN),
            P(CHAN),
            P(CHAN, None),
        ),
        out_specs=P(AXES, None),
        check_vma=False,
    )
```

```python
import functools
import itertools

import jax
import jax.numpy as jnp
import ml_dtypes
import numpy as np
from jax import lax
from jax.experimental import pallas as pl
from jax.experimental.pallas import tpu as pltpu
from jax.sharding import Mesh
from jax.sharding import PartitionSpec as P


SIZES = {"y": 4, "zl": 2, "core": 2, "x": 4, "zh": 2}
AXES = tuple(SIZES)
SEQ, CHAN = ("y", "zl", "core"), ("x", "zh")

N1 = 128
HALF = 72
CH = 16
BF, F32 = jnp.bfloat16, jnp.float32


def split_np(array):
    high = array.astype(np.float32).astype(ml_dtypes.bfloat16)
    low = (array - high.astype(np.float64)).astype(np.float32).astype(ml_dtypes.bfloat16)
    return high, low


@functools.cache
def tables():
    full = 2 * 8192
    freq = np.arange(HALF)[:, None]
    valid = (freq <= N1 // 2).astype(np.float64)
    block = np.arange(64)[None, :]
    angle = 2 * np.pi * (freq * block % N1) / N1
    first = np.concatenate([np.cos(angle) * valid, -np.sin(angle) * valid], 0)
    high, low = split_np(first)
    zero = np.zeros_like(high)
    first_signal = np.concatenate([high, high, low, zero], 1)
    rank = np.arange(64)
    order = 4 * (rank % 16) + rank // 16
    first_filter = np.concatenate([high[:, order], low[:, order]], 1)
    lane = np.arange(128)[None, :]
    turn = 2 * np.pi * (freq * lane) / full
    twiddle = np.stack([np.cos(turn) * valid, -np.sin(turn) * valid]).astype(np.float32)
    pair = 2 * np.pi * (np.arange(128)[:, None] * lane % 128) / 128
    cosine, sine = np.cos(pair), np.sin(pair)
    second = np.concatenate(
        [np.concatenate([cosine, -sine], 1), np.concatenate([sine, cosine], 1)], 0
    )
    second = np.stack(split_np(second))
    weight = np.where((freq == 0) | (freq == N1 // 2), 1.0, 2.0) * valid / full
    last = np.concatenate([np.cos(angle) * weight, -np.sin(angle) * weight], 0).T
    high, low = split_np(last)
    last = np.concatenate([high, high, low, np.zeros((64, 80), high.dtype)], 1)
    return first_signal, first_filter, twiddle, second, last


def halves(value):
    high = value.astype(BF)
    return high, (value - high.astype(F32)).astype(BF)


def mm(left, right, dims=(((1,), (0,)), ((), ()))):
    return lax.dot_general(left, right, dims, preferred_element_type=F32)


def in_hbm(array):
    return pltpu.with_memory_space_constraint(array, pltpu.HBM)


def seq_index():
    return (lax.axis_index("y") * 2 + lax.axis_index("zl")) * 2 + lax.axis_index("core")


def column_index():
    return lax.rem(lax.axis_index("y"), 2) * 2 + lax.axis_index("zl")


def pack_kernel(filt_hbm, tokens_hbm, weight_hbm, payload, held, filt, tokens, sems):
    parts = 2
    mine = weight_hbm.at[
        :,
        pl.ds(pl.multiple_of(lax.axis_index("core") * CH, CH), CH),
        pl.ds(pl.multiple_of(column_index() * 1024, 1024), 1024),
    ]
    rows = 512 // parts
    copies = [
        pltpu.make_async_copy(filt_hbm.at[i * rows : (i + 1) * rows], filt.at[i * rows : (i + 1) * rows], sems.at[i])
        for i in range(parts)
    ]
    copies.append(pltpu.make_async_copy(tokens_hbm, tokens, sems.at[parts]))
    copies.append(pltpu.make_async_copy(mine, held, sems.at[parts + 1]))
    for copy in copies:
        copy.start()
    copies[parts].wait()
    high = jnp.right_shift(tokens[...], 4)
    low = jnp.bitwise_and(tokens[...], 15)
    gap = jnp.zeros((4, 128), F32)
    digits = jnp.concatenate([high.astype(F32), gap, low.astype(F32), gap], 0).astype(BF)
    payload[:, :, 512:] = jnp.broadcast_to(digits[None], (16, CH, 128))
    for i in range(parts):
        copies[i].wait()
        at = slice(i * rows, (i + 1) * rows)
        payload[:, :, at] = filt[at, :].T.astype(BF).reshape(16, CH, rows)
    copies[parts + 1].wait()


def pack(long_filter, token_ids, out_weight):
    hbm, whole = pl.BlockSpec(memory_space=pltpu.HBM), pl.BlockSpec(memory_space=pltpu.VMEM)
    return pl.pallas_call(
        pack_kernel,
        out_shape=(
            jax.ShapeDtypeStruct((16, CH, 640), BF),
            jax.ShapeDtypeStruct((8, CH, 1024), BF),
        ),
        in_specs=[hbm] * 3,
        out_specs=(whole, whole),
        scratch_shapes=[
            pltpu.VMEM((512, 256), F32),
            pltpu.VMEM((4, 128), jnp.int32),
            pltpu.SemaphoreType.DMA((4,)),
        ],
        cost_estimate=pl.CostEstimate(flops=1 << 18, bytes_accessed=1 << 20, transcendentals=0),
        compiler_params=pltpu.CompilerParams(vmem_limit_bytes=6 << 20),
        name="pack",
    )(in_hbm(long_filter), in_hbm(token_ids.reshape(4, 128)), in_hbm(out_weight.reshape(8, 2 * CH, 4096)))


STEPS = 4
GROUP = 8
BATCH = 4
UNROLL = 4


def vocab_kernel(embed_hbm, weight_hbm, table, embed, weight, sems):
    depth = 4096 // STEPS
    lanes = pl.ds(pl.multiple_of(lax.div(seq_index(), 8) * 128, 128), 128)
    copies = []
    for step in range(STEPS):
        at = slice(step * depth, (step + 1) * depth)
        pair = [pltpu.make_async_copy(embed_hbm.at[:, at], embed.at[:, at], sems.at[4 * step + 3])]
        for branch in range(3):
            pair.append(
                pltpu.make_async_copy(
                    weight_hbm.at[branch, at, lanes],
                    weight.at[at, branch * 128 : (branch + 1) * 128],
                    sems.at[4 * step + branch],
                )
            )
        copies.append(pair)
    for pair in copies:
        for copy in pair:
            copy.start()
    total = None
    for step, pair in enumerate(copies):
        for copy in pair:
            copy.wait()
        at = slice(step * depth, (step + 1) * depth)
        part = mm(embed[:, at], weight[at, :])
        total = part if total is None else total + part
    lane = lax.broadcasted_iota(jnp.int32, (CH, 128), 1)
    row = lax.broadcasted_iota(jnp.int32, (CH, 128), 0)
    pick = (lane == row + CH * lax.rem(seq_index(), 8)).astype(F32).astype(BF)
    for branch in range(3):
        rows = total[:, branch * 128 : (branch + 1) * 128].astype(BF)
        table[branch * CH : (branch + 1) * CH, :] = mm(pick, rows, (((1,), (1,)), ((), ())))


def vocab(embed_table, in_weight):
    hbm = pl.BlockSpec(memory_space=pltpu.HBM)
    return pl.pallas_call(
        vocab_kernel,
        out_shape=jax.ShapeDtypeStruct((3 * CH, 512), F32),
        in_specs=[hbm, hbm],
        out_specs=pl.BlockSpec(memory_space=pltpu.VMEM),
        scratch_shapes=[
            pltpu.VMEM((512, 4096), BF),
            pltpu.VMEM((4096, 384), BF),
            pltpu.SemaphoreType.DMA((4 * STEPS,)),
        ],
        compiler_params=pltpu.CompilerParams(vmem_limit_bytes=16 << 20),
        cost_estimate=pl.CostEstimate(flops=2 * 512 * 4096 * 384, bytes_accessed=8 << 20, transcendentals=0),
        name="vocab",
    )(in_hbm(embed_table), in_hbm(in_weight.transpose(1, 0, 2)))


def convolve_kernel(
    recv, table, *refs,
):
    sources, (out, taps, token, gated, other, shaped, spec_high, spec_low, lags) = refs[:7], refs[7:16]
    short, direct, first_signal, first_filter, twiddle, second, last = held = refs[16:23]
    chunk, out_sems = refs[24:]
    copies = [
        pltpu.make_async_copy(source, target, refs[23].at[index])
        for index, (source, target) in enumerate(zip(sources, held))
    ]
    for copy in copies:
        copy.start()
    for source in range(16):
        digits = recv[source, :, 512:].astype(F32)
        token[source * 8 : source * 8 + 8, :] = (digits[:8] * 16.0 + digits[8:]).astype(jnp.int32)
        for q in range(4):
            rows = slice(q * 256 + source * CH, q * 256 + (source + 1) * CH)
            lags[rows, :] = recv[source, :, q * 128 : (q + 1) * 128].astype(F32)

    banks = jnp.concatenate([table[:, i * 128 : (i + 1) * 128] for i in range(4)], 0).astype(BF)
    line = lax.broadcasted_iota(jnp.int32, (256, 256), 0)
    lane = lax.broadcasted_iota(jnp.int32, (256, 256), 1)
    shift = (line == jnp.where(lane < 128, lane + 127, lane - 2)).astype(F32).astype(BF)
    entry = lax.broadcasted_iota(jnp.int32, (128, 128), 0)

    copies[0].wait()
    copies[1].wait()
    seq, core = seq_index(), lax.axis_index("core")
    lane = lax.broadcasted_iota(jnp.int32, (CH, 256), 1)
    row = lax.broadcasted_iota(jnp.int32, (CH, 256), 0)
    mine = lane == row + CH * seq
    for index in range(10):
        wide = short[index // 3, index % 3 : index % 3 + 1, :] if index < 9 else direct[...]
        column = jnp.sum(jnp.where(mine, wide, 0.0), axis=1, keepdims=True)
        taps[index * CH : (index + 1) * CH, :] = jnp.broadcast_to(column, (CH, 128))

    def select(step, before):
        blocks = [before]
        for source in range(BATCH):
            rows = [token[pl.ds((step * BATCH + source) * 8 + q, 1), :] for q in range(4)]
            chosen = [(entry == jnp.bitwise_and(row, 127)).astype(F32).astype(BF) for row in rows]
            found = mm(banks, jnp.concatenate(chosen, 1))
            bank = jnp.right_shift(jnp.concatenate(rows, 1), 7)
            value = found[: 3 * CH]
            for i in range(1, 4):
                value = jnp.where(bank == i, found[i * 3 * CH : (i + 1) * 3 * CH], value)
            narrow = value.astype(BF)
            blocks += [narrow[:, q * 128 : (q + 1) * 128] for q in range(4)]
        pairs = [jnp.concatenate([blocks[q], blocks[q + 1]], 1) for q in range(4 * BATCH)]
        lagged = mm(jnp.concatenate(pairs, 0), shift)
        for q in range(4 * BATCH):
            lag = lagged[q * 3 * CH : (q + 1) * 3 * CH]
            filtered = taps[: 3 * CH, :] * blocks[q + 1].astype(F32)
            filtered = filtered + taps[3 * CH : 6 * CH, :] * lag[:, :128]
            filtered = filtered + taps[6 * CH : 9 * CH, :] * lag[:, 128:]
            at = pl.ds(pl.multiple_of((step * 4 * BATCH + q) * CH, CH), CH)
            gated[at, :] = filtered[:CH] * filtered[2 * CH :]
            other[at, :] = filtered[CH : 2 * CH]
        return blocks[-1]

    lax.fori_loop(0, 16 // BATCH, select, jnp.zeros((3 * CH, 128), BF), unroll=UNROLL)

    for copy in copies[2:]:
        copy.wait()
    cos_turn, sin_turn = twiddle[0], twiddle[1]
    rows_all = CH * HALF

    def turned(stage, sign):
        real, imag = stage[:HALF], stage[HALF:]
        return jnp.concatenate(
            [real * cos_turn - sign * imag * sin_turn, sign * real * sin_turn + imag * cos_turn], 1
        )

    for pair in range(CH // 2):
        signal = jnp.concatenate(
            [gated[pl.ds(2 * pair + i, 64, stride=CH), :] for i in range(2)], 1
        )
        high, low = halves(signal)
        stage = mm(first_signal[...], jnp.concatenate([high, low, high, high], 0))
        spectrum = jnp.concatenate([turned(stage[:, :128], 1), turned(stage[:, 128:], 1)], 0)
        at = slice(pair * 2 * HALF, (pair + 1) * 2 * HALF)
        spec_high[at, :], spec_low[at, :] = halves(spectrum)

        kernel = jnp.concatenate(
            [lags[pl.ds(2 * pair + i, 64, stride=CH), :] for i in range(2)], 1
        ).astype(BF)
        stage = mm(first_filter[...], jnp.concatenate([kernel, kernel], 0))
        spectrum = jnp.concatenate([turned(stage[:, :128], 1), turned(stage[:, 128:], 1)], 0)
        at = slice(rows_all + pair * 2 * HALF, rows_all + (pair + 1) * 2 * HALF)
        spec_high[at, :], spec_low[at, :] = halves(spectrum)

    def transform(at, dims):
        high, low = spec_high[at, :], spec_low[at, :]
        return mm(high, second[0], dims) + (mm(low, second[0], dims) + mm(high, second[1], dims))

    straight, flipped = (((1,), (0,)), ((), ())), (((1,), (1,)), ((), ()))
    span = 2 * HALF
    for start in range(0, CH // 2, GROUP):
        at = slice(start * span, (start + GROUP) * span)
        left = transform(at, straight)
        right = transform(slice(rows_all + at.start, rows_all + at.stop), straight)
        left_real, left_imag, right_real, right_imag = left[:, :128], left[:, 128:], right[:, :128], right[:, 128:]
        product = jnp.concatenate(
            [left_real * right_real - left_imag * right_imag, left_real * right_imag + left_imag * right_real], 1
        )
        spec_high[at, :], spec_low[at, :] = halves(product)

    for start in range(0, CH // 2, GROUP):
        backs = transform(slice(start * span, (start + GROUP) * span), flipped)
        for pair in range(start, start + GROUP):
            columns = []
            for i in range(2):
                top = ((pair - start) * 2 + i) * HALF
                real, imag = backs[top : top + HALF, :128], backs[top : top + HALF, 128:]
                columns.append(
                    jnp.concatenate([real * cos_turn + imag * sin_turn, imag * cos_turn - real * sin_turn], 0)
                )
            high, low = halves(jnp.concatenate(columns, 1))
            result = mm(last[...], jnp.concatenate([high, low, high, high[:80]], 0))
            for i in range(2):
                shaped[pl.ds(2 * pair + i, 64, stride=CH), :] = result[:, i * 128 : (i + 1) * 128]

    skip = taps[9 * CH :, :]
    low_half = lax.broadcasted_iota(jnp.int32, (CH, 128), 1) < 64
    copies = []
    for a, h in itertools.product(range(2), range(4)):
        for top, core_to in itertools.product(range(2), range(2)):
            done = []
            for zl in range(2):
                shard = 8 * a + top * 4 + zl * 2 + core_to
                rows = slice((4 * shard + h) * CH, (4 * shard + h + 1) * CH)
                done.append(other[rows, :] * (shaped[rows, :] + skip * gated[rows, :]))
            first, then = done
            half = jnp.bitwise_xor(core, core_to) if core_to else core
            columns = pl.ds(pl.multiple_of(half * 256 + top * 128, 128), 128)
            chunk[a * 8 + 2 * h, :, columns] = jnp.where(low_half, first, pltpu.roll(then, 64, 1)).astype(BF)
            chunk[a * 8 + 2 * h + 1, :, columns] = jnp.where(low_half, pltpu.roll(first, 64, 1), then).astype(BF)
        for member in range(4):
            copies.append(
                pltpu.make_async_copy(
                    chunk.at[a * 8 + 2 * h : a * 8 + 2 * h + 2],
                    out.at[pl.ds((a * 4 + member) * 8 + 2 * h, 2)],
                    out_sems.at[(a * 4 + h) * 4 + member],
                )
            )
            copies[-1].start()
    for copy in copies:
        copy.wait()


def convolve(recv, table, short_filter, skip_gain):
    consts = [jnp.asarray(c) for c in tables()]
    whole, hbm = pl.BlockSpec(memory_space=pltpu.VMEM), pl.BlockSpec(memory_space=pltpu.HBM)
    positions = 8192
    fetched = [short_filter, skip_gain[None, :], *consts]
    return pl.pallas_call(
        convolve_kernel,
        out_shape=pltpu.HBM((64, CH, 512), BF),
        in_specs=[whole] * 2 + [hbm] * 7,
        out_specs=hbm,
        scratch_shapes=[
            pltpu.VMEM((10 * CH, 128), F32),
            pltpu.VMEM((128, 128), jnp.int32),
            pltpu.VMEM((positions // 128 * CH, 128), F32),
            pltpu.VMEM((positions // 128 * CH, 128), F32),
            pltpu.VMEM((positions // 128 * CH, 128), F32),
            pltpu.VMEM((2 * CH * HALF, 256), BF),
            pltpu.VMEM((2 * CH * HALF, 256), BF),
            pltpu.VMEM((64 * CH, 128), F32),
            *[pltpu.VMEM(array.shape, array.dtype) for array in fetched],
            pltpu.SemaphoreType.DMA((len(fetched),)),
            pltpu.VMEM((16, CH, 512), BF),
            pltpu.SemaphoreType.DMA((32,)),
        ],
        cost_estimate=pl.CostEstimate(flops=4 << 30, bytes_accessed=4 << 20, transcendentals=0),
        compiler_params=pltpu.CompilerParams(vmem_limit_bytes=20 << 20),
        name="convolve",
    )(recv, table, *[in_hbm(array) for array in fetched])


def project_kernel(half, recv, own, one, upper, lower, three, out):
    chan = lax.axis_index("x") * 2 + lax.axis_index("zh")
    total = None
    for index in range(4):
        lhs = jnp.concatenate(
            [
                recv[:, jnp.bitwise_xor(chan, 2 * index + i), :, half * 256 : (half + 1) * 256].reshape(128, 256)
                for i in range(2)
            ],
            0,
        )
        rhs = jnp.concatenate([upper[...], lower[...]], 0) if index == 2 else (own, one, None, three)[index][...]
        part = mm(lhs, rhs, (((0,), (0,)), ((), ())))
        total = part if total is None else total + part
    out[...] = total.astype(out.dtype)


def project(recv, weights, half):
    whole = pl.BlockSpec(memory_space=pltpu.VMEM)
    return pl.pallas_call(
        functools.partial(project_kernel, half),
        out_shape=jax.ShapeDtypeStruct((256, 1024), BF if half else F32),
        in_specs=[whole] * 6,
        out_specs=whole,
        cost_estimate=pl.CostEstimate(flops=1 << 29, bytes_accessed=4 << 20, transcendentals=0),
        compiler_params=pltpu.CompilerParams(vmem_limit_bytes=20 << 20),
        name="send" if half else "keep",
    )(recv.reshape(8, 8, CH, 512), *weights)


def combine_kernel(keep, came, *outs):
    for index, out in enumerate(outs):
        block = jnp.bitwise_xor(column_index(), index)
        rows = pl.ds(pl.multiple_of(block * 64, 64), 64)
        out[...] = (keep[rows, :] + came[rows, :].astype(F32)).astype(BF)


def combine(keep, came):
    whole = pl.BlockSpec(memory_space=pltpu.VMEM)
    return pl.pallas_call(
        combine_kernel,
        out_shape=(jax.ShapeDtypeStruct((64, 1024), BF),) * 4,
        in_specs=[whole, whole],
        out_specs=(whole,) * 4,
        cost_estimate=pl.CostEstimate(flops=1 << 18, bytes_accessed=2 << 20, transcendentals=0),
        compiler_params=pltpu.CompilerParams(vmem_limit_bytes=6 << 20),
        name="combine",
    )(keep, came)


def assemble_kernel(first, *refs):
    pieces, out, sems = refs[: -2], refs[-2], refs[-1]
    pieces = pieces if first == 0 else pieces[:-1]
    copies = []
    for index, piece in enumerate(pieces):
        block = jnp.bitwise_xor(column_index(), first + index)
        columns = pl.ds(pl.multiple_of(block * 1024, 1024), 1024)
        copies.append(pltpu.make_async_copy(piece, out.at[:, columns], sems.at[index]))
        copies[-1].start()
    for copy in copies:
        copy.wait()


def assemble(pieces, first=0, into=None):
    anywhere = pl.BlockSpec(memory_space=pl.ANY)
    operands = list(pieces) + ([] if into is None else [into])
    return pl.pallas_call(
        functools.partial(assemble_kernel, first),
        out_shape=jax.ShapeDtypeStruct((64, 4096), BF),
        in_specs=[anywhere] * len(operands),
        out_specs=anywhere,
        scratch_shapes=[pltpu.SemaphoreType.DMA((len(pieces),))],
        input_output_aliases={} if into is None else {len(pieces): 0},
        cost_estimate=pl.CostEstimate(flops=0, bytes_accessed=1 << 20, transcendentals=0),
        compiler_params=pltpu.CompilerParams(vmem_limit_bytes=4 << 20),
        name="assemble" if into is None else "finish",
    )(*operands)


def permuted(block, move):
    pairs = []
    for place in itertools.product(*[range(SIZES[axis]) for axis in AXES]):
        here = dict(zip(AXES, place))
        there = {**here, **move(here)}
        index = [0, 0]
        for axis in AXES:
            index = [index[0] * SIZES[axis] + here[axis], index[1] * SIZES[axis] + there[axis]]
        pairs.append(tuple(index))
    return lax.ppermute(block, AXES, pairs)


def body(token_ids, embed_table, in_weight, short_filter, long_filter, skip_gain, out_weight):
    payload, held = pack(long_filter, token_ids, out_weight)
    held = held.reshape(128, 1024)
    across = permuted(held, lambda d: {"zh": d["zh"] ^ 1})
    both = jnp.concatenate([held, across], 0)
    beside = {}
    for index in (1, 3):
        beside[index] = permuted(both, lambda d: {"x": d["x"] ^ index})
    recv = lax.all_to_all(payload, SEQ, 0, 0, tiled=True)
    table = vocab(embed_table, in_weight)
    chunks = convolve(recv, table, short_filter, skip_gain)
    recv = lax.all_to_all(chunks, ("y", "zl", "x", "zh"), 0, 0, tiled=True)
    upper = permuted(beside[3][:128], lambda d: {"x": d["x"] ^ 1})
    lower = permuted(beside[1][128:], lambda d: {"x": d["x"] ^ 3})
    weights = [both, beside[1], upper, lower, beside[3]]
    send = project(recv, weights, 1)
    came = permuted(send, lambda d: {"core": 1 - d["core"]})
    keep = project(recv, weights, 0)
    pieces = list(combine(keep, came))
    for index in range(1, 4):
        pieces[index] = permuted(pieces[index], lambda d: {"y": d["y"] ^ (index // 2), "zl": d["zl"] ^ (index % 2)})
    most = assemble(pieces[:3])
    return assemble(pieces[3:], 3, most)


def solution(mesh):
    fine = Mesh(mesh.devices.reshape(tuple(SIZES.values())), AXES)
    return jax.shard_map(
        body,
        mesh=fine,
        in_specs=(
            P(SEQ),
            P(),
            P(None, None, CHAN),
            P(None, None, CHAN),
            P(SEQ, CHAN),
            P(CHAN),
            P(CHAN, None),
        ),
        out_specs=P(AXES, None),
        check_vma=False,
    )
```
